128 devices in a mesh: scan: 4 (over y_lo, core), ybrick: 32 (over y_hi, x, z).
Axes of the slice: x: 4, y: 4 (y_hi: 2, y_lo: 2; y = y_hi * 2 + y_lo), z: 4, core: 2. Of those that a mesh axis runs over, the one named last changes fastest.
Arguments:
- raw: bfloat16 [16, 4096, 2048], P(None, 'ybrick', 'scan'), may hold values from 0.099609375 to 4
- row_shift: int32 [16], replicated, may hold values from 0 to 1023
- frac_index: int32 [16], replicated, may hold values from 0 to 15
- psf_y: float32 [65], replicated, may hold values from 0.05 to 1
- psf_x: float32 [65], replicated, may hold values from 0.05 to 1
Outputs:
- estimate: float32 [16, 4096, 2048], P('scan', 'ybrick')
The draws below stay inside these ranges and needn't reach their ends.
All inputs are finite; a program needn't handle non-finite values.
Results may differ from the reference program's by a relative error of at most 0.0021.
Values may be sent and summed in bfloat16 or wider, within the bound.
A program may use at most 128 MiB of HBM per device.

```python
import math
import jax
import jax.numpy as jnp
from jax import lax

X = 2048
RADIUS = 32
ITERS = 2
NFRAC = 16
TAPS = 65
Y = 4096
P_SIZE = 16


def place_ends(values, key, smallest, high):
    longest = values.shape.index(max(values.shape))
    spots = []
    for shift in (0, 1):
        where = [jax.random.randint(jax.random.fold_in(key, axis), (), 0, length) for axis, length in enumerate(values.shape)]
        where[longest] = (where[longest] + shift) % values.shape[longest]
        spots.append(tuple(where))
    return values.at[spots[0]].set(smallest).at[spots[1]].set(high)


def level_of(stream_key, shape, shards, smallest, largest):
    def one(position, shards_of):
        draws = jax.random.uniform(jax.random.fold_in(jax.random.fold_in(stream_key, 6), position), (shards_of,), jnp.float32, smallest / len(shards), largest / len(shards))
        return jnp.repeat(jnp.exp(draws), shape[position] // shards_of).reshape((-1,) + (1,) * (len(shape) - position - 1))

    gain = one(*shards[0])
    for cut in shards[1:]:
        gain = gain * one(*cut)
    return gain


def setup_inputs(seed: int = 0) -> dict:
    streams_of = jax.random.split(jax.random.key(seed), 6)
    raw = jnp.clip(jnp.exp(math.log(4.0) - 3.6927934 * jax.random.uniform(streams_of[0], (P_SIZE, Y, X), jnp.float32) ** level_of(streams_of[0], (P_SIZE, Y, X), ((1, 32), (2, 4)), -0.2, 0.2)), 0.099609375, 4.0).astype(jnp.bfloat16)
    row_shift = place_ends(jax.random.randint(streams_of[1], (P_SIZE,), 0, Y // 4), jax.random.fold_in(streams_of[1], 1), 0, (Y // 4) - 1).astype(jnp.int32)
    frac_index = place_ends(jax.random.randint(streams_of[2], (P_SIZE,), 0, NFRAC), jax.random.fold_in(streams_of[2], 1), 0, NFRAC - 1).astype(jnp.int32)
    psf_y = jnp.clip(jnp.exp(jax.random.uniform(streams_of[3], (TAPS,), jnp.float32, math.log(0.05), math.log(1.0))), 0.05, 1.0)
    psf_x = jnp.clip(jnp.exp(jax.random.uniform(streams_of[4], (TAPS,), jnp.float32, math.log(0.05), math.log(1.0))), 0.05, 1.0)
    return {"raw": raw, "row_shift": row_shift, "frac_index": frac_index, "psf_y": psf_y, "psf_x": psf_x}


background = 0.5


def deskew_frame(frame_data, shift, fraction):
    height, width = frame_data.shape
    weight = fraction.astype(jnp.float32) / NFRAC
    padded = jnp.concatenate([jnp.zeros((height + 1, width), jnp.float32), frame_data.astype(jnp.float32)], axis=0)
    upper = lax.dynamic_slice_in_dim(padded, (height + 1 - shift).astype(jnp.int32), height, 0)
    lower = lax.dynamic_slice_in_dim(padded, (height - shift).astype(jnp.int32), height, 0)
    return ((1.0 - weight) * upper + weight * lower).astype(jnp.bfloat16)


def line_filter(source, kernel):
    result = lax.conv_general_dilated(source[:, None, :], kernel[None, None, :], (1,), [(RADIUS, RADIUS)], dimension_numbers=("NCH", "OIH", "NCH"), precision=lax.Precision.HIGHEST)
    return result[:, 0, :]


def reference(raw, row_shift, frac_index, psf_y, psf_x):
    kernel_y = psf_y / jnp.sum(psf_y)
    kernel_x = psf_x / jnp.sum(psf_x)

    def per_plane(inputs):
        frame_data, shift, fraction = inputs
        observed = deskew_frame(frame_data, shift, fraction).astype(jnp.float32) + background
        estimate = observed
        for turn_index in range(ITERS):
            blurred = line_filter(line_filter(estimate.T, kernel_y).T, kernel_x)
            ratio = observed / blurred
            correction = line_filter(line_filter(ratio, kernel_x[::-1]).T, kernel_y[::-1]).T
            estimate = estimate * correction
        return estimate

    return lax.map(per_plane, (raw, row_shift, frac_index))
```

```python
import functools

import jax
import jax.numpy as jnp
from jax import lax
from jax.experimental import pallas as pl
from jax.experimental.pallas import tpu as pltpu
from jax.sharding import PartitionSpec as P

RADIUS = 32
TAPS = 2 * RADIUS + 1
ITERS = 2
NFRAC = 16
BRICK = 128
BRICKS = 32
COLS = 512
HALO = 2 * ITERS * RADIUS
REACH = 8
HALF = 16
WINDOW = HALF + 1
SLOTS = WINDOW + REACH
ROWS = WINDOW * BRICK
WIDE = COLS + 2 * HALO
STEP = 192
SPAN = STEP + 2 * RADIUS
BLOCK = 2 * STEP
PADDED = 6 * BLOCK
TINY = 1e-30

background = 0.5


def toeplitz(kernel, count_out, count_in):
    padded = jnp.pad(kernel, (0, count_in + 1 - TAPS))
    return jnp.tile(padded, count_out)[: count_out * count_in].reshape(count_out, count_in)


def rows_band(kernel):
    return toeplitz(kernel, STEP, SPAN).astype(jnp.bfloat16)


def columns_band(kernel):
    band = toeplitz(kernel, 256, 416)
    return jnp.pad(band, ((0, 0), (96, 0))).T.astype(jnp.bfloat16)


def deskew_kernel(scalars, raw_ref, out_ref, buffer):
    half, shift = scalars[0], scalars[1]
    weight = scalars[2].astype(jnp.float32) / NFRAC

    def widen(k, carry):
        brick = k - REACH + (HALF - 1) * half
        tile = raw_ref[jnp.maximum(brick, 0)].astype(jnp.float32)
        buffer[pl.ds(pl.multiple_of(k * BRICK, BRICK), BRICK), :] = jnp.where(brick >= 0, tile, 0.0)
        return carry

    lax.fori_loop(0, SLOTS, widen, 0)

    def blend(i, carry):
        start = REACH * BRICK + BRICK * i - shift - 1
        rest = lax.rem(start, 8)
        tall = BRICK + 16
        rows = buffer[pl.ds(pl.multiple_of(start - rest, 8), tall), :]
        lower = pltpu.roll(rows, lax.rem(tall - rest, tall), 0)[:BRICK]
        upper = pltpu.roll(rows, tall - 1 - rest, 0)[:BRICK]
        mixed = (1.0 - weight) * upper + weight * lower
        out_ref[pl.ds(pl.multiple_of(i * BRICK, BRICK), BRICK), :] = mixed.astype(jnp.bfloat16)
        return carry

    lax.fori_loop(0, WINDOW, blend, 0)


def filter_kernel(
    scalars, left, middle, right, y_forward, y_back, x_forward, x_back, out_ref, observed, estimate, rounded, back, rows_done, ratio
):
    half, scan = scalars[0], scalars[1]
    zeros = jnp.zeros((RADIUS, WIDE), jnp.bfloat16)
    for ref in (rounded, back):
        ref[pl.ds(0, RADIUS), :] = zeros
        ref[pl.ds(RADIUS + PADDED, RADIUS), :] = zeros
    tail = PADDED - ROWS
    observed[pl.ds(ROWS, tail), :] = jnp.zeros((tail, WIDE), jnp.float32)
    rounded[pl.ds(RADIUS + ROWS, tail), :] = jnp.zeros((tail, WIDE), jnp.bfloat16)

    def load(i, carry):
        rows = pl.ds(pl.multiple_of(i * BRICK, BRICK), BRICK)
        target = pl.ds(pl.multiple_of(i * BRICK + RADIUS, RADIUS), BRICK)
        for ref, first, width, inside in (
            (left, 0, HALO, scan > 0),
            (middle, HALO, COLS, None),
            (right, HALO + COLS, HALO, scan < 3),
        ):
            values = ref[rows, :].astype(jnp.float32) + background
            if inside is not None:
                values = jnp.where(inside, values, 0.0)
            observed[rows, pl.ds(first, width)] = values
            rounded[target, pl.ds(first, width)] = values.astype(jnp.bfloat16)
        return carry

    lax.fori_loop(0, WINDOW, load, 0)

    windows = ((0, 384, 128), (128, 640, 0), (384, 768, 0))

    def columns(source, band, block):
        low, high, offset = windows[block]
        return jnp.dot(
            source[:, low:high], band[offset : offset + high - low, :], preferred_element_type=jnp.float32
        )

    def forward(i, carry):
        base = i * BLOCK
        for q in range(2):
            window = rounded[pl.ds(pl.multiple_of(base + q * STEP, 64), SPAN), :]
            rows_done[pl.ds(q * STEP, STEP), :] = jnp.dot(
                y_forward[...], window, preferred_element_type=jnp.float32
            ).astype(jnp.bfloat16)
        rows = pl.ds(pl.multiple_of(base, BLOCK), BLOCK)
        for block in range(3):
            blurred = columns(rows_done, x_forward, block)
            seen = observed[rows, pl.ds(block * 256, 256)]
            ratio[:, pl.ds(block * 256, 256)] = (seen / jnp.maximum(blurred, TINY)).astype(jnp.bfloat16)
        target = pl.ds(pl.multiple_of(base + RADIUS, RADIUS), BLOCK)
        for block in range(3):
            back[target, pl.ds(block * 256, 256)] = columns(ratio, x_back, block).astype(jnp.bfloat16)
        return carry

    def update(i, carry):
        base = pl.multiple_of(i * STEP, STEP)
        correction = jnp.dot(y_back[...], back[pl.ds(base, SPAN), :], preferred_element_type=jnp.float32)
        fresh = observed[pl.ds(base, STEP), :] * correction
        estimate[pl.ds(base, STEP), :] = fresh
        rounded[pl.ds(pl.multiple_of(base + RADIUS, RADIUS), STEP), :] = fresh.astype(jnp.bfloat16)
        return carry

    def finish(i, carry):
        base = jnp.minimum(i * STEP, HALF * BRICK - STEP)
        source = pl.multiple_of(base + BRICK * half, 64)
        correction = jnp.dot(
            y_back[...], back[pl.ds(source, SPAN), pl.ds(HALO, COLS)], preferred_element_type=jnp.float32
        )
        final = estimate[pl.ds(source, STEP), pl.ds(HALO, COLS)] * correction
        out_ref[pl.ds(pl.multiple_of(base, 64), STEP), :] = (final * final).astype(jnp.bfloat16)
        return carry

    lax.fori_loop(0, PADDED // BLOCK, forward, 0)
    lax.fori_loop(0, PADDED // STEP, update, 0)
    lax.fori_loop(0, PADDED // BLOCK, forward, 0)
    lax.fori_loop(0, -(-HALF * BRICK // STEP), finish, 0)


SMEM = pl.BlockSpec(memory_space=pltpu.SMEM)
VMEM = pl.BlockSpec(memory_space=pltpu.VMEM)


def deskew(half, shift, fraction, raw):
    return pl.pallas_call(
        deskew_kernel,
        out_shape=jax.ShapeDtypeStruct((ROWS, COLS), jnp.bfloat16),
        in_specs=[SMEM, VMEM],
        out_specs=VMEM,
        scratch_shapes=[pltpu.VMEM((SLOTS * BRICK + 16, COLS), jnp.float32)],
        compiler_params=pltpu.CompilerParams(vmem_limit_bytes=60 * 2**20),
    )(jnp.stack([half, shift, fraction]), raw)


def deconvolve(half, scan, left, middle, right, kernel_y, kernel_x):
    return pl.pallas_call(
        filter_kernel,
        out_shape=jax.ShapeDtypeStruct((HALF * BRICK, COLS), jnp.bfloat16),
        in_specs=[SMEM] + [VMEM] * 7,
        out_specs=VMEM,
        scratch_shapes=[
            pltpu.VMEM((PADDED, WIDE), jnp.float32),
            pltpu.VMEM((PADDED, WIDE), jnp.float32),
            pltpu.VMEM((PADDED + 2 * RADIUS, WIDE), jnp.bfloat16),
            pltpu.VMEM((PADDED + 2 * RADIUS, WIDE), jnp.bfloat16),
            pltpu.VMEM((BLOCK, WIDE), jnp.bfloat16),
            pltpu.VMEM((BLOCK, WIDE), jnp.bfloat16),
        ],
        compiler_params=pltpu.CompilerParams(vmem_limit_bytes=60 * 2**20),
    )(
        jnp.stack([half, scan]),
        left,
        middle,
        right,
        rows_band(kernel_y),
        rows_band(kernel_y[::-1]),
        columns_band(kernel_x),
        columns_band(kernel_x[::-1]),
    )


def local(raw, row_shift, frac_index, psf_y, psf_x):
    scan = lax.axis_index("scan").astype(jnp.int32)
    spot = lax.axis_index("ybrick").astype(jnp.int32)
    half, plane = spot // HALF, spot % HALF
    gathered = lax.all_to_all(jnp.concatenate([raw, raw], axis=0), "ybrick", split_axis=0, concat_axis=0, tiled=True)
    shift = lax.dynamic_index_in_dim(row_shift, plane, keepdims=False)
    fraction = lax.dynamic_index_in_dim(frac_index, plane, keepdims=False)
    middle = deskew(half, shift, fraction, gathered)
    left = lax.ppermute(middle[:, COLS - HALO :], "scan", [(i, i + 1) for i in range(3)])
    right = lax.ppermute(middle[:, :HALO], "scan", [(i + 1, i) for i in range(3)])
    kernel_y = psf_y / jnp.sum(psf_y)
    kernel_x = psf_x / jnp.sum(psf_x)
    coded = deconvolve(half, scan, left, middle, right, kernel_y, kernel_x).reshape(HALF, BRICK, COLS)
    groups = [list(range(HALF)), list(range(HALF, 2 * HALF))]
    coded = lax.all_to_all(coded, "ybrick", split_axis=0, concat_axis=0, axis_index_groups=groups, tiled=True)
    coded = lax.all_to_all(coded, "scan", split_axis=0, concat_axis=2, tiled=True)
    return jnp.sqrt(coded.astype(jnp.float32))


def solution(mesh):
    return jax.shard_map(
        local,
        mesh=mesh,
        in_specs=(P(None, "ybrick", "scan"), P(), P(), P(), P()),
        out_specs=P("scan", "ybrick", None),
        check_vma=False,
    )
```

```python
import functools

import jax
import jax.numpy as jnp
from jax import lax
from jax.experimental import pallas as pl
from jax.experimental.pallas import tpu as pltpu
from jax.sharding import PartitionSpec as P

RADIUS = 32
TAPS = 2 * RADIUS + 1
ITERS = 2
NFRAC = 16
BRICK = 128
BRICKS = 32
COLS = 512
HALO = 2 * ITERS * RADIUS
REACH = 8
HALF = 16
WINDOW = HALF + 1
SLOTS = WINDOW + REACH
ROWS = WINDOW * BRICK
WIDE = COLS + 2 * HALO
STEP = 192
SPAN = STEP + 2 * RADIUS
BLOCK = 2 * STEP
PADDED = 6 * BLOCK
TINY = 1e-30

background = 0.5


def toeplitz(kernel, count_out, count_in):
    padded = jnp.pad(kernel, (0, count_in + 1 - TAPS))
    return jnp.tile(padded, count_out)[: count_out * count_in].reshape(count_out, count_in)


def rows_band(kernel):
    return toeplitz(kernel, STEP, SPAN).astype(jnp.bfloat16)


def columns_band(kernel):
    band = toeplitz(kernel, 256, 416)
    return jnp.pad(band, ((0, 0), (96, 0))).T.astype(jnp.bfloat16)


def deskew_kernel(scalars, raw_ref, out_ref, buffer):
    half, shift = scalars[0], scalars[1]
    weight = scalars[2].astype(jnp.float32) / NFRAC

    def widen(k, carry):
        inside = k + (HALF - 1) * half >= REACH
        buffer[pl.ds(pl.multiple_of(k * BRICK, BRICK), BRICK), :] = jnp.where(inside, raw_ref[k].astype(jnp.float32), 0.0)
        return carry

    lax.fori_loop(0, SLOTS, widen, 0)

    def blend(i, carry):
        start = REACH * BRICK + BRICK * i - shift - 1
        rest = lax.rem(start, 8)
        tall = BRICK + 16
        rows = buffer[pl.ds(pl.multiple_of(start - rest, 8), tall), :]
        lower = pltpu.roll(rows, lax.rem(tall - rest, tall), 0)[:BRICK]
        upper = pltpu.roll(rows, tall - 1 - rest, 0)[:BRICK]
        mixed = (1.0 - weight) * upper + weight * lower
        out_ref[pl.ds(pl.multiple_of(i * BRICK, BRICK), BRICK), :] = mixed.astype(jnp.bfloat16)
        return carry

    lax.fori_loop(0, WINDOW, blend, 0)


def filter_kernel(
    scalars, left, middle, right, y_forward, y_back, x_forward, x_back, out_ref, observed, estimate, rounded, back, rows_done, ratio
):
    half, scan = scalars[0], scalars[1]
    zeros = jnp.zeros((RADIUS, WIDE), jnp.bfloat16)
    for ref in (rounded, back):
        ref[pl.ds(0, RADIUS), :] = zeros
        ref[pl.ds(RADIUS + PADDED, RADIUS), :] = zeros
    tail = PADDED - ROWS
    observed[pl.ds(ROWS, tail), :] = jnp.zeros((tail, WIDE), jnp.float32)
    rounded[pl.ds(RADIUS + ROWS, tail), :] = jnp.zeros((tail, WIDE), jnp.bfloat16)

    def load(i, carry):
        rows = pl.ds(pl.multiple_of(i * BRICK, BRICK), BRICK)
        target = pl.ds(pl.multiple_of(i * BRICK + RADIUS, RADIUS), BRICK)
        for ref, first, width, inside in (
            (left, 0, HALO, scan > 0),
            (middle, HALO, COLS, None),
            (right, HALO + COLS, HALO, scan < 3),
        ):
            values = ref[rows, :].astype(jnp.float32) + background
            if inside is not None:
                values = jnp.where(inside, values, 0.0)
            observed[rows, pl.ds(first, width)] = values
            rounded[target, pl.ds(first, width)] = values.astype(jnp.bfloat16)
        return carry

    lax.fori_loop(0, WINDOW, load, 0)

    windows = ((0, 384, 128), (128, 640, 0), (384, 768, 0))

    def columns(source, band, block):
        low, high, offset = windows[block]
        return jnp.dot(
            source[:, low:high], band[offset : offset + high - low, :], preferred_element_type=jnp.float32
        )

    def forward(i, carry):
        base = i * BLOCK
        for q in range(2):
            window = rounded[pl.ds(pl.multiple_of(base + q * STEP, 64), SPAN), :]
            rows_done[pl.ds(q * STEP, STEP), :] = jnp.dot(
                y_forward[...], window, preferred_element_type=jnp.float32
            ).astype(jnp.bfloat16)
        rows = pl.ds(pl.multiple_of(base, BLOCK), BLOCK)
        for block in range(3):
            blurred = columns(rows_done, x_forward, block)
            seen = observed[rows, pl.ds(block * 256, 256)]
            ratio[:, pl.ds(block * 256, 256)] = (seen / jnp.maximum(blurred, TINY)).astype(jnp.bfloat16)
        target = pl.ds(pl.multiple_of(base + RADIUS, RADIUS), BLOCK)
        for block in range(3):
            back[target, pl.ds(block * 256, 256)] = columns(ratio, x_back, block).astype(jnp.bfloat16)
        return carry

    def update(i, carry):
        base = pl.multiple_of(i * STEP, STEP)
        correction = jnp.dot(y_back[...], back[pl.ds(base, SPAN), :], preferred_element_type=jnp.float32)
        fresh = observed[pl.ds(base, STEP), :] * correction
        estimate[pl.ds(base, STEP), :] = fresh
        rounded[pl.ds(pl.multiple_of(base + RADIUS, RADIUS), STEP), :] = fresh.astype(jnp.bfloat16)
        return carry

    def finish(i, carry):
        base = jnp.minimum(i * STEP, HALF * BRICK - STEP)
        source = pl.multiple_of(base + BRICK * half, 64)
        correction = jnp.dot(
            y_back[...], back[pl.ds(source, SPAN), pl.ds(HALO, COLS)], preferred_element_type=jnp.float32
        )
        final = estimate[pl.ds(source, STEP), pl.ds(HALO, COLS)] * correction
        out_ref[pl.ds(pl.multiple_of(base, 64), STEP), :] = (final * final).astype(jnp.bfloat16)
        return carry

    lax.fori_loop(0, PADDED // BLOCK, forward, 0)
    lax.fori_loop(0, PADDED // STEP, update, 0)
    lax.fori_loop(0, PADDED // BLOCK, forward, 0)
    lax.fori_loop(0, -(-HALF * BRICK // STEP), finish, 0)


MESH = pl.DeviceIdType.MESH
REFS = pl.BlockSpec(memory_space=pl.ANY)
BOTH_FIRST, BOTH_LAST = HALF - 1 - REACH, HALF


def slot_of(brick, half):
    return brick + REACH - (HALF - 1) * half


def gather_kernel(raw, slots, send, recv, own):
    scan, brick = lax.axis_index("scan"), lax.axis_index("ybrick")
    mine_half, mine = brick // HALF, brick % HALF

    def device(index):
        return {"scan": scan, "ybrick": index}

    barrier = pltpu.get_barrier_semaphore()
    first = (BOTH_FIRST) * mine_half
    last = BOTH_LAST + (BRICKS - 1 - BOTH_LAST) * mine_half

    def greet(index, carry):
        @pl.when(index != brick)
        def _():
            pl.semaphore_signal(barrier, inc=1, device_id=device(index), device_id_type=MESH)

        return carry

    lax.fori_loop(first, last + 1, greet, 0)
    to_zero = (brick <= BOTH_LAST).astype(jnp.int32)
    to_one = (brick >= BOTH_FIRST).astype(jnp.int32)
    pl.semaphore_wait(barrier, HALF * (to_zero + to_one) - 1)

    keep = pltpu.make_async_copy(raw.at[mine], slots.at[slot_of(brick, mine_half)], own)
    keep.start()

    def copy(step, half):
        plane = lax.rem(mine + step, HALF)
        slot = slot_of(brick, half)
        return pltpu.make_async_remote_copy(
            src_ref=raw.at[plane],
            dst_ref=slots.at[slot],
            send_sem=send.at[half, plane],
            recv_sem=recv.at[slot],
            device_id=device(half * HALF + plane),
            device_id_type=MESH,
        )

    def each(act):
        def body(step, carry):
            for half, goes in ((0, to_zero), (1, to_one)):

                @pl.when((goes == 1) & ((step > 0) | (mine_half != half)))
                def _():
                    act(copy(step, half))

            return carry

        lax.fori_loop(0, HALF, body, 0)

    each(lambda one: one.start())

    def arrive(index, carry):
        @pl.when(index != brick)
        def _():
            slot = slot_of(index, mine_half)
            pltpu.make_async_copy(slots.at[slot], slots.at[slot], recv.at[slot]).wait()

        return carry

    keep.wait()
    lax.fori_loop(first, last + 1, arrive, 0)
    each(lambda one: one.wait_send())


def gather(raw):
    return pl.pallas_call(
        gather_kernel,
        out_shape=jax.ShapeDtypeStruct((SLOTS, BRICK, COLS), jnp.bfloat16),
        in_specs=[REFS],
        out_specs=REFS,
        scratch_shapes=[
            pltpu.SemaphoreType.DMA((2, HALF)),
            pltpu.SemaphoreType.DMA((SLOTS,)),
            pltpu.SemaphoreType.DMA,
        ],
        compiler_params=pltpu.CompilerParams(collective_id=0, has_side_effects=True),
    )(raw)


def scatter_kernel(coded, whole, send, recv, own):
    scan, spot = lax.axis_index("scan"), lax.axis_index("ybrick")
    half, plane = spot // HALF, spot % HALF
    group, place = plane // 4, lax.rem(plane, 4)
    barrier = pltpu.get_barrier_semaphore()

    def greet(index, carry):
        source_scan, source_plane = index // 4, scan * 4 + lax.rem(index, 4)

        @pl.when((source_scan != scan) | (source_plane != plane))
        def _():
            pl.semaphore_signal(
                barrier,
                inc=1,
                device_id={"scan": source_scan, "ybrick": half * HALF + source_plane},
                device_id_type=MESH,
            )

        return carry

    lax.fori_loop(0, HALF, greet, 0)
    stays = (group == scan).astype(jnp.int32)
    pl.semaphore_wait(barrier, HALF - stays)

    def target(place, scan):
        return whole.at[place, :, pl.ds(pl.multiple_of(scan * COLS, COLS), COLS)]

    def copy(step):
        tile = lax.rem(plane + step, HALF)
        return pltpu.make_async_remote_copy(
            src_ref=coded.at[tile],
            dst_ref=target(place, scan),
            send_sem=send.at[tile],
            recv_sem=recv.at[place, scan],
            device_id={"scan": group, "ybrick": half * HALF + tile},
            device_id_type=MESH,
        )

    keep = pltpu.make_async_copy(coded.at[plane], target(place, scan), own)

    @pl.when(stays == 1)
    def _():
        keep.start()

    def each(act):
        def body(step, carry):
            @pl.when((step > 0) | (stays == 0))
            def _():
                act(copy(step))

            return carry

        lax.fori_loop(0, HALF, body, 0)

    each(lambda one: one.start())

    @pl.when(stays == 1)
    def _():
        keep.wait()

    def arrive(index, carry):
        source_scan, slot = index // 4, lax.rem(index, 4)

        @pl.when((source_scan != scan) | (scan * 4 + slot != plane))
        def _():
            pltpu.make_async_copy(target(slot, source_scan), target(slot, source_scan), recv.at[slot, source_scan]).wait()

        return carry

    lax.fori_loop(0, HALF, arrive, 0)
    each(lambda one: one.wait_send())


def scatter(coded):
    return pl.pallas_call(
        scatter_kernel,
        out_shape=jax.ShapeDtypeStruct((4, BRICK, 4 * COLS), jnp.bfloat16),
        in_specs=[REFS],
        out_specs=REFS,
        scratch_shapes=[
            pltpu.SemaphoreType.DMA((HALF,)),
            pltpu.SemaphoreType.DMA((4, 4)),
            pltpu.SemaphoreType.DMA,
        ],
        compiler_params=pltpu.CompilerParams(collective_id=1, has_side_effects=True),
    )(coded)


def decode_kernel(coded, out):
    out[...] = jnp.sqrt(coded[...].astype(jnp.float32))


def decode(coded):
    return pl.pallas_call(
        decode_kernel,
        grid=(8,),
        out_shape=jax.ShapeDtypeStruct(coded.shape, jnp.float32),
        in_specs=[pl.BlockSpec((4, 16, 4 * COLS), lambda i: (0, i, 0))],
        out_specs=pl.BlockSpec((4, 16, 4 * COLS), lambda i: (0, i, 0)),
    )(coded)


SMEM = pl.BlockSpec(memory_space=pltpu.SMEM)
VMEM = pl.BlockSpec(memory_space=pltpu.VMEM)


def deskew(half, shift, fraction, raw):
    return pl.pallas_call(
        deskew_kernel,
        out_shape=jax.ShapeDtypeStruct((ROWS, COLS), jnp.bfloat16),
        in_specs=[SMEM, VMEM],
        out_specs=VMEM,
        scratch_shapes=[pltpu.VMEM((SLOTS * BRICK + 16, COLS), jnp.float32)],
        compiler_params=pltpu.CompilerParams(vmem_limit_bytes=60 * 2**20),
    )(jnp.stack([half, shift, fraction]), raw)


def deconvolve(half, scan, left, middle, right, kernel_y, kernel_x):
    return pl.pallas_call(
        filter_kernel,
        out_shape=jax.ShapeDtypeStruct((HALF * BRICK, COLS), jnp.bfloat16),
        in_specs=[SMEM] + [VMEM] * 7,
        out_specs=VMEM,
        scratch_shapes=[
            pltpu.VMEM((PADDED, WIDE), jnp.float32),
            pltpu.VMEM((PADDED, WIDE), jnp.float32),
            pltpu.VMEM((PADDED + 2 * RADIUS, WIDE), jnp.bfloat16),
            pltpu.VMEM((PADDED + 2 * RADIUS, WIDE), jnp.bfloat16),
            pltpu.VMEM((BLOCK, WIDE), jnp.bfloat16),
            pltpu.VMEM((BLOCK, WIDE), jnp.bfloat16),
        ],
        compiler_params=pltpu.CompilerParams(vmem_limit_bytes=60 * 2**20),
    )(
        jnp.stack([half, scan]),
        left,
        middle,
        right,
        rows_band(kernel_y),
        rows_band(kernel_y[::-1]),
        columns_band(kernel_x),
        columns_band(kernel_x[::-1]),
    )


def local(raw, row_shift, frac_index, psf_y, psf_x):
    scan = lax.axis_index("scan").astype(jnp.int32)
    spot = lax.axis_index("ybrick").astype(jnp.int32)
    half, plane = spot // HALF, spot % HALF
    gathered = gather(raw)
    shift = lax.dynamic_index_in_dim(row_shift, plane, keepdims=False)
    fraction = lax.dynamic_index_in_dim(frac_index, plane, keepdims=False)
    middle = deskew(half, shift, fraction, gathered)
    left = lax.ppermute(middle[:, COLS - HALO :], "scan", [(i, i + 1) for i in range(3)])
    right = lax.ppermute(middle[:, :HALO], "scan", [(i + 1, i) for i in range(3)])
    kernel_y = psf_y / jnp.sum(psf_y)
    kernel_x = psf_x / jnp.sum(psf_x)
    coded = deconvolve(half, scan, left, middle, right, kernel_y, kernel_x).reshape(HALF, BRICK, COLS)
    return decode(scatter(coded))


def solution(mesh):
    return jax.shard_map(
        local,
        mesh=mesh,
        in_specs=(P(None, "ybrick", "scan"), P(), P(), P(), P()),
        out_specs=P("scan", "ybrick", None),
        check_vma=False,
    )
```

```python
import functools

import jax
import jax.numpy as jnp
from jax import lax
from jax.experimental import pallas as pl
from jax.experimental.pallas import tpu as pltpu
from jax.sharding import PartitionSpec as P

RADIUS = 32
TAPS = 2 * RADIUS + 1
NFRAC = 16
BRICK = 128
BRICKS = 32
ROWS = BRICK * BRICKS
REACH = 1024
PART = 256
HALO = 128
WIDE = PART + 2 * HALO
SPAN = BRICK + 2 * RADIUS
UNIT = 2
TALL = UNIT * BRICK
BLOCKS = BRICKS // UNIT
STRIDE = 7
TINY = 1e-30
MESH = pl.DeviceIdType.MESH
SMEM = pl.BlockSpec(memory_space=pltpu.SMEM)
VMEM = pl.BlockSpec(memory_space=pltpu.VMEM)
REFS = pl.BlockSpec(memory_space=pl.ANY)

background = 0.5


def spot_of(plane, side, scan):
    deep, down, high = plane // 8, (plane // 2) % 4, plane % 2
    return high * 16 + down * 4 + (2 * deep + scan + side) % 4


def work_of(scan, ybrick):
    turn = (ybrick % 4 - scan + 4) % 4
    return 8 * (turn // 2) + 2 * ((ybrick % 16) // 4) + ybrick // 16, turn % 2


def toeplitz(kernel, count_out, count_in):
    padded = jnp.pad(kernel, (0, count_in + 1 - TAPS))
    return jnp.tile(padded, count_out)[: count_out * count_in].reshape(count_out, count_in)


def rows_band(kernel):
    return toeplitz(kernel, BRICK, SPAN).astype(jnp.bfloat16)


def columns_band(kernel):
    band = toeplitz(kernel, PART, 416)
    return jnp.pad(band, ((0, 0), (96, 0))).T.astype(jnp.bfloat16)


def gather_kernel(raw, slots, send, recv, own):
    scan, brick = lax.axis_index("scan"), lax.axis_index("ybrick")
    barrier = pltpu.get_barrier_semaphore()

    def greet(step, carry):
        other = (brick + step) % BRICKS
        pl.semaphore_signal(barrier, inc=1, device_id={"ybrick": other}, device_id_type=MESH)
        return carry

    lax.fori_loop(1, BRICKS, greet, 0)
    pl.semaphore_wait(barrier, BRICKS - 1)

    def source(spot):
        plane, side = work_of(scan, spot)
        return raw.at[plane, :, pl.ds(pl.multiple_of(side * PART, PART), PART)]

    keep = pltpu.make_async_copy(source(brick), slots.at[brick], own)
    keep.start()

    def copy(step):
        spot = (brick + STRIDE * step) % BRICKS
        return pltpu.make_async_remote_copy(
            src_ref=source(spot),
            dst_ref=slots.at[brick],
            send_sem=send.at[spot],
            recv_sem=recv.at[brick],
            device_id={"ybrick": spot},
            device_id_type=MESH,
        )

    def start(step, carry):
        copy(step).start()
        return carry

    def arrive(step, carry):
        slot = (brick + step) % BRICKS
        pltpu.make_async_copy(slots.at[slot], slots.at[slot], recv.at[slot]).wait()
        return carry

    def sent(step, carry):
        copy(step).wait_send()
        return carry

    lax.fori_loop(1, BRICKS, start, 0)
    keep.wait()
    lax.fori_loop(1, BRICKS, arrive, 0)
    lax.fori_loop(1, BRICKS, sent, 0)


def gather(raw):
    return pl.pallas_call(
        gather_kernel,
        out_shape=jax.ShapeDtypeStruct((BRICKS, BRICK, PART), jnp.bfloat16),
        in_specs=[REFS],
        out_specs=REFS,
        scratch_shapes=[
            pltpu.SemaphoreType.DMA((BRICKS,)),
            pltpu.SemaphoreType.DMA((BRICKS,)),
            pltpu.SemaphoreType.DMA,
        ],
        compiler_params=pltpu.CompilerParams(collective_id=0, has_side_effects=True),
    )(raw)


def deskew_kernel(scalars, raw, out, buffer):
    shift = scalars[0]
    weight = scalars[1].astype(jnp.float32) / NFRAC

    def clear(k, carry):
        buffer[pl.ds(pl.multiple_of(k * BRICK, BRICK), BRICK), :] = jnp.zeros((BRICK, PART), jnp.float32)
        return carry

    def widen(k, carry):
        target = pl.ds(pl.multiple_of(REACH + k * BRICK, BRICK), BRICK)
        buffer[target, :] = raw[k].astype(jnp.float32)
        return carry

    def blend(k, carry):
        start = REACH + BRICK * k - shift - 1
        rest = lax.rem(start, 8)
        tall = BRICK + 16
        rows = buffer[pl.ds(pl.multiple_of(start - rest, 8), tall), :]
        lower = pltpu.roll(rows, lax.rem(tall - rest, tall), 0)[:BRICK]
        upper = pltpu.roll(rows, tall - 1 - rest, 0)[:BRICK]
        mixed = (1.0 - weight) * upper + weight * lower
        out[pl.ds(pl.multiple_of(k * BRICK, BRICK), BRICK), :] = mixed.astype(jnp.bfloat16)
        return carry

    lax.fori_loop(0, REACH // BRICK, clear, 0)
    lax.fori_loop(0, BRICKS, widen, 0)
    lax.fori_loop(0, BRICKS, blend, 0)


def deskew(shift, fraction, raw):
    return pl.pallas_call(
        deskew_kernel,
        out_shape=jax.ShapeDtypeStruct((ROWS, PART), jnp.bfloat16),
        in_specs=[SMEM, VMEM],
        out_specs=VMEM,
        scratch_shapes=[pltpu.VMEM((REACH + ROWS + 16, PART), jnp.float32)],
        compiler_params=pltpu.CompilerParams(vmem_limit_bytes=60 * 2**20),
    )(jnp.stack([shift, fraction]), raw)


def filter_kernel(
    middle, y_forward, y_back, x_forward, x_back, whole,
    observed, estimate, rounded, back, rows_done, ratio, coded, left, right,
    halo_send, halo_recv, send, recv, own,
):
    scan, spot = lax.axis_index("scan"), lax.axis_index("ybrick")
    plane, side = work_of(scan, spot)
    group, part = plane // 4, 2 * scan + side
    stays = (group == scan).astype(jnp.int32)
    first = ((plane % 4) * 8 + part) // UNIT
    has_left, has_right = part > 0, part < 7

    def owner(plane, part):
        return {"scan": part // 2, "ybrick": spot_of(plane, part % 2, part // 2)}

    barrier = pltpu.get_barrier_semaphore()

    def greet(index, carry):
        other, column = scan * 4 + index // 8, index % 8

        @pl.when((other != plane) | (column != part))
        def _():
            pl.semaphore_signal(barrier, inc=1, device_id=owner(other, column), device_id_type=MESH)

        return carry

    for there, step in ((has_left, -1), (has_right, 1)):

        @pl.when(there)
        def _():
            pl.semaphore_signal(barrier, inc=1, device_id=owner(plane, part + step), device_id_type=MESH)

    lax.fori_loop(0, BRICKS, greet, 0)
    pl.semaphore_wait(barrier, BRICKS - stays + has_left.astype(jnp.int32) + has_right.astype(jnp.int32))

    def block_at(turn):
        return (first + turn + BLOCKS) % BLOCKS

    def rows_of(block, offset=0):
        return pl.ds(pl.multiple_of(block * TALL + offset, RADIUS), TALL)

    def halo(block, to_right):
        edge = middle.at[rows_of(block), pl.ds(HALO if to_right else 0, HALO)]
        return pltpu.make_async_remote_copy(
            src_ref=edge,
            dst_ref=(left if to_right else right).at[rows_of(block), :],
            send_sem=halo_send.at[int(to_right), block],
            recv_sem=halo_recv.at[int(to_right), block],
            device_id=owner(plane, part + (1 if to_right else -1)),
            device_id_type=MESH,
        )

    def each_halo(act):
        def body(turn, carry):
            for there, to_right in ((has_left, False), (has_right, True)):

                @pl.when(there)
                def _():
                    act(halo(block_at(turn - 1), to_right))

            return carry

        lax.fori_loop(0, BLOCKS, body, 0)

    each_halo(lambda one: one.start())
    zeros = jnp.zeros((RADIUS, WIDE), jnp.bfloat16)
    for ref in (rounded, back):
        ref[pl.ds(0, RADIUS), :] = zeros
        ref[pl.ds(RADIUS + ROWS, RADIUS), :] = zeros

    def load(block):
        rows = rows_of(block)
        for ref, arrived, at, width, inside in (
            (middle, None, HALO, PART, None),
            (left, 1, 0, HALO, has_left),
            (right, 0, HALO + PART, HALO, has_right),
        ):
            if arrived is not None:

                @pl.when(inside)
                def _():
                    pltpu.make_async_copy(ref.at[rows, :], ref.at[rows, :], halo_recv.at[arrived, block]).wait()

            values = ref[rows, :].astype(jnp.float32) + background
            if inside is not None:
                values = jnp.where(inside, values, 0.0)
            observed[rows, pl.ds(at, width)] = values
            rounded[rows_of(block, RADIUS), pl.ds(at, width)] = values.astype(jnp.bfloat16)

    def dot(one, two):
        return jnp.dot(one, two, preferred_element_type=jnp.float32)

    def window(block, unit):
        return pl.ds(pl.multiple_of(block * TALL + unit * BRICK, BRICK), SPAN)

    blocks = ((0, 384, 128), (128, 512, 0))

    def ratios(block):
        for unit in range(UNIT):
            rows_done[pl.ds(unit * BRICK, BRICK), :] = dot(
                y_forward[...], rounded[window(block, unit), :]
            ).astype(jnp.bfloat16)
        for at, (low, high, offset) in enumerate(blocks):
            blurred = dot(rows_done[:, low:high], x_forward[offset : offset + high - low, :])
            cut = pl.ds(at * PART, PART)
            ratio[:, cut] = (observed[rows_of(block), cut] / jnp.maximum(blurred, TINY)).astype(jnp.bfloat16)

    def forward(block):
        ratios(block)
        for at, (low, high, offset) in enumerate(blocks):
            turned = dot(ratio[:, low:high], x_back[offset : offset + high - low, :])
            back[rows_of(block, RADIUS), pl.ds(at * PART, PART)] = turned.astype(jnp.bfloat16)

    def update(block):
        for unit in range(UNIT):
            rows = pl.ds(pl.multiple_of(block * TALL + unit * BRICK, BRICK), BRICK)
            fresh = observed[rows, :] * dot(y_back[...], back[window(block, unit), :])
            estimate[rows, :] = fresh[:, HALO : HALO + PART]
            target = pl.ds(pl.multiple_of(block * TALL + unit * BRICK + RADIUS, RADIUS), BRICK)
            rounded[target, :] = fresh.astype(jnp.bfloat16)

    def again(block):
        ratios(block)
        back[rows_of(block, RADIUS), pl.ds(HALO, PART)] = dot(ratio[...], x_back[...]).astype(jnp.bfloat16)

    def finish(block):
        for unit in range(UNIT):
            rows = pl.ds(pl.multiple_of(block * TALL + unit * BRICK, BRICK), BRICK)
            correction = dot(y_back[...], back[window(block, unit), pl.ds(HALO, PART)])
            final = estimate[rows, :] * correction
            coded[block * UNIT + unit] = (final * final).astype(jnp.bfloat16)

    def target(place, part):
        return whole.at[place, :, pl.ds(pl.multiple_of(part * PART, PART), PART)]

    keep = pltpu.make_async_copy(coded.at[spot], target(plane % 4, part), own)

    def leave(brick):
        return pltpu.make_async_remote_copy(
            src_ref=coded.at[brick],
            dst_ref=target(plane % 4, part),
            send_sem=send.at[brick],
            recv_sem=recv.at[plane % 4, part],
            device_id={"scan": group, "ybrick": brick},
            device_id_type=MESH,
        )

    def ship(block):
        for unit in range(UNIT):
            brick = block * UNIT + (unit + part) % UNIT
            away = (stays == 0) | (brick != spot)

            @pl.when(away)
            def _():
                leave(brick).start()

            @pl.when(jnp.logical_not(away))
            def _():
                keep.start()

    load(block_at(-1))
    load(block_at(0))

    def step(turn, carry):
        for stage, lag, begin, end in (
            (load, -1, 0, BLOCKS - 3),
            (forward, 0, 0, BLOCKS - 1),
            (update, 1, 2, BLOCKS + 1),
            (again, 2, 4, BLOCKS + 3),
            (ship, 4, 7, BLOCKS + 6),
            (finish, 3, 6, BLOCKS + 5),
        ):

            @pl.when((turn >= begin) & (turn <= end))
            def _():
                stage(block_at(turn - lag))

        return carry

    lax.fori_loop(0, BLOCKS + 7, step, 0)

    @pl.when(stays == 1)
    def _():
        keep.wait()

    def arrive(index, carry):
        other, column = scan * 4 + index // 8, index % 8

        @pl.when((other != plane) | (column != part))
        def _():
            ref = target(index // 8, column)
            pltpu.make_async_copy(ref, ref, recv.at[index // 8, column]).wait()

        return carry

    lax.fori_loop(0, BRICKS, arrive, 0)

    def sent(brick, carry):
        @pl.when((stays == 0) | (brick != spot))
        def _():
            leave(brick).wait_send()

        return carry

    lax.fori_loop(0, BRICKS, sent, 0)
    each_halo(lambda one: one.wait_send())


def deconvolve(middle, kernel_y, kernel_x):
    return pl.pallas_call(
        filter_kernel,
        out_shape=jax.ShapeDtypeStruct((4, BRICK, 8 * PART), jnp.bfloat16),
        in_specs=[VMEM] * 5,
        out_specs=REFS,
        scratch_shapes=[
            pltpu.VMEM((ROWS, WIDE), jnp.float32),
            pltpu.VMEM((ROWS, PART), jnp.float32),
            pltpu.VMEM((ROWS + 2 * RADIUS, WIDE), jnp.bfloat16),
            pltpu.VMEM((ROWS + 2 * RADIUS, WIDE), jnp.bfloat16),
            pltpu.VMEM((TALL, WIDE), jnp.bfloat16),
            pltpu.VMEM((TALL, WIDE), jnp.bfloat16),
            pltpu.VMEM((BRICKS, BRICK, PART), jnp.bfloat16),
            pltpu.VMEM((ROWS, HALO), jnp.bfloat16),
            pltpu.VMEM((ROWS, HALO), jnp.bfloat16),
            pltpu.SemaphoreType.DMA((2, BLOCKS)),
            pltpu.SemaphoreType.DMA((2, BLOCKS)),
            pltpu.SemaphoreType.DMA((BRICKS,)),
            pltpu.SemaphoreType.DMA((4, 8)),
            pltpu.SemaphoreType.DMA,
        ],
        compiler_params=pltpu.CompilerParams(
            collective_id=1, has_side_effects=True, vmem_limit_bytes=60 * 2**20
        ),
    )(
        middle,
        rows_band(kernel_y),
        rows_band(kernel_y[::-1]),
        columns_band(kernel_x),
        columns_band(kernel_x[::-1]),
    )


def decode_kernel(coded, out):
    values = coded[...].astype(jnp.float32)
    out[...] = values * lax.rsqrt(values)


def decode(coded):
    spec = pl.BlockSpec((4, 16, 8 * PART), lambda i: (0, i, 0))
    return pl.pallas_call(
        decode_kernel,
        grid=(BRICK // 16,),
        out_shape=jax.ShapeDtypeStruct(coded.shape, jnp.float32),
        in_specs=[spec],
        out_specs=spec,
    )(coded)


def local(raw, row_shift, frac_index, psf_y, psf_x):
    scan = lax.axis_index("scan").astype(jnp.int32)
    spot = lax.axis_index("ybrick").astype(jnp.int32)
    plane, _ = work_of(scan, spot)
    shift = lax.dynamic_index_in_dim(row_shift, plane, keepdims=False)
    fraction = lax.dynamic_index_in_dim(frac_index, plane, keepdims=False)
    middle = deskew(shift, fraction, gather(raw))
    kernel_y = psf_y / jnp.sum(psf_y)
    kernel_x = psf_x / jnp.sum(psf_x)
    return decode(deconvolve(middle, kernel_y, kernel_x))


def solution(mesh):
    return jax.shard_map(
        local,
        mesh=mesh,
        in_specs=(P(None, "ybrick", "scan"), P(), P(), P(), P()),
        out_specs=P("scan", "ybrick", None),
        check_vma=False,
    )
```

```python
import functools

import jax
import jax.numpy as jnp
from jax import lax
from jax.experimental import pallas as pl
from jax.experimental.pallas import tpu as pltpu
from jax.sharding import PartitionSpec as P

RADIUS = 32
TAPS = 2 * RADIUS + 1
NFRAC = 16
BRICK = 128
BRICKS = 32
ROWS = BRICK * BRICKS
REACH = 1024
PART = 256
HALO = 128
WIDE = PART + 2 * HALO
SPAN = BRICK + 2 * RADIUS
UNIT = 2
TALL = UNIT * BRICK
BLOCKS = BRICKS // UNIT
STRIDE = 7
TINY = 1e-30
MESH = pl.DeviceIdType.MESH
SMEM = pl.BlockSpec(memory_space=pltpu.SMEM)
VMEM = pl.BlockSpec(memory_space=pltpu.VMEM)
REFS = pl.BlockSpec(memory_space=pl.ANY)

background = 0.5


def spot_of(plane, side, scan):
    deep, down, high = plane // 8, (plane // 2) % 4, plane % 2
    return high * 16 + down * 4 + (2 * deep + scan + side) % 4


def work_of(scan, ybrick):
    turn = (ybrick % 4 - scan + 4) % 4
    return 8 * (turn // 2) + 2 * ((ybrick % 16) // 4) + ybrick // 16, turn % 2


def start_of(scan, ybrick):
    plane, side = work_of(scan, ybrick)
    high, down = ybrick // 16, (ybrick // 4) % 2
    return (5 * ((plane % 4) * 8 + 2 * scan + side)) % 32


def spread(line, height, width, first):
    rows = jnp.broadcast_to(line[:, :width], (height, width))
    return pltpu.roll(rows, first % width, 1, stride=1, stride_axis=0)


def bands(psf_y, psf_x, line, y_forward, y_back, x_forward, x_back):
    line[...] = jnp.zeros_like(line)
    line[:, :TAPS] = psf_y[...] / jnp.sum(psf_y[...], axis=1, keepdims=True)
    y_forward[...] = spread(line, BRICK, 2 * BRICK, 0)[:, :SPAN].astype(jnp.bfloat16)
    turned = spread(line, 2 * BRICK, 2 * BRICK, -2 * RADIUS)[:, :BRICK].T
    y_back[...] = turned[:, :SPAN].astype(jnp.bfloat16)
    line[:, :TAPS] = psf_x[...] / jnp.sum(psf_x[...], axis=1, keepdims=True)
    x_forward[...] = spread(line, PART, WIDE, HALO - RADIUS).T.astype(jnp.bfloat16)
    x_back[...] = spread(line, WIDE, WIDE, -(HALO + RADIUS))[:, :PART].astype(jnp.bfloat16)


def gather_kernel(raw, psf_y, psf_x, slots, y_forward, y_back, x_forward, x_back, line, send, recv, own):
    scan, brick = lax.axis_index("scan"), lax.axis_index("ybrick")
    barrier = pltpu.get_barrier_semaphore()

    def greet(step, carry):
        other = (brick + step) % BRICKS
        pl.semaphore_signal(barrier, inc=1, device_id={"ybrick": other}, device_id_type=MESH)
        return carry

    lax.fori_loop(1, BRICKS, greet, 0)
    pl.semaphore_wait(barrier, BRICKS - 1)

    def source(spot):
        plane, side = work_of(scan, spot)
        return raw.at[plane, :, pl.ds(pl.multiple_of(side * PART, PART), PART)]

    keep = pltpu.make_async_copy(source(brick), slots.at[brick], own)
    keep.start()

    def copy(step):
        spot = (brick + STRIDE * step) % BRICKS
        return pltpu.make_async_remote_copy(
            src_ref=source(spot),
            dst_ref=slots.at[brick],
            send_sem=send.at[spot],
            recv_sem=recv.at[brick],
            device_id={"ybrick": spot},
            device_id_type=MESH,
        )

    def start(step, carry):
        copy(step).start()
        return carry

    def arrive(step, carry):
        slot = (brick + step) % BRICKS
        pltpu.make_async_copy(slots.at[slot], slots.at[slot], recv.at[slot]).wait()
        return carry

    def sent(step, carry):
        copy(step).wait_send()
        return carry

    lax.fori_loop(1, BRICKS, start, 0)
    bands(psf_y, psf_x, line, y_forward, y_back, x_forward, x_back)
    keep.wait()
    lax.fori_loop(1, BRICKS, arrive, 0)
    lax.fori_loop(1, BRICKS, sent, 0)


def gather(raw, psf_y, psf_x):
    return pl.pallas_call(
        gather_kernel,
        out_shape=[
            jax.ShapeDtypeStruct(shape, jnp.bfloat16)
            for shape in ((BRICKS, BRICK, PART), (BRICK, SPAN), (BRICK, SPAN), (WIDE, PART), (WIDE, PART))
        ],
        in_specs=[REFS, VMEM, VMEM],
        out_specs=[REFS] + [VMEM] * 4,
        scratch_shapes=[
            pltpu.VMEM((1, WIDE), jnp.float32),
            pltpu.SemaphoreType.DMA((BRICKS,)),
            pltpu.SemaphoreType.DMA((BRICKS,)),
            pltpu.SemaphoreType.DMA,
        ],
        compiler_params=pltpu.CompilerParams(collective_id=0, has_side_effects=True),
    )(raw, psf_y.reshape(1, TAPS), psf_x.reshape(1, TAPS))


def deskew_kernel(row_shift, frac_index, raw, out, buffer):
    plane, _ = work_of(lax.axis_index("scan"), lax.axis_index("ybrick"))
    shift = row_shift[plane]
    weight = frac_index[plane].astype(jnp.float32) / NFRAC

    def clear(k, carry):
        buffer[pl.ds(pl.multiple_of(k * BRICK, BRICK), BRICK), :] = jnp.zeros((BRICK, PART), jnp.float32)
        return carry

    def widen(k, carry):
        target = pl.ds(pl.multiple_of(REACH + k * BRICK, BRICK), BRICK)
        buffer[target, :] = raw[k].astype(jnp.float32)
        return carry

    def blend(k, carry):
        start = REACH + BRICK * k - shift - 1
        rest = lax.rem(start, 8)
        tall = BRICK + 16
        rows = buffer[pl.ds(pl.multiple_of(start - rest, 8), tall), :]
        lower = pltpu.roll(rows, lax.rem(tall - rest, tall), 0)[:BRICK]
        upper = pltpu.roll(rows, tall - 1 - rest, 0)[:BRICK]
        mixed = (1.0 - weight) * upper + weight * lower
        out[pl.ds(pl.multiple_of(k * BRICK, BRICK), BRICK), :] = mixed.astype(jnp.bfloat16)
        return carry

    lax.fori_loop(0, REACH // BRICK, clear, 0)
    lax.fori_loop(0, BRICKS, widen, 0)
    lax.fori_loop(0, BRICKS, blend, 0)


def deskew(row_shift, frac_index, raw):
    return pl.pallas_call(
        deskew_kernel,
        out_shape=jax.ShapeDtypeStruct((ROWS, PART), jnp.bfloat16),
        in_specs=[SMEM, SMEM, VMEM],
        out_specs=VMEM,
        scratch_shapes=[pltpu.VMEM((REACH + ROWS + 16, PART), jnp.float32)],
        compiler_params=pltpu.CompilerParams(vmem_limit_bytes=60 * 2**20),
    )(row_shift, frac_index, raw)


def filter_kernel(
    middle, y_forward, y_back, x_forward, x_back, whole,
    observed, estimate, rounded, back, rounded_2, back_2, rows_done, ratio, rows_done_2, ratio_2,
    coded, left, right,
    halo_send, halo_recv, send, recv, own,
):
    scan, spot = lax.axis_index("scan"), lax.axis_index("ybrick")
    plane, side = work_of(scan, spot)
    group, part = plane // 4, 2 * scan + side
    stays = (group == scan).astype(jnp.int32)
    first = start_of(scan, spot) // UNIT
    has_left, has_right = part > 0, part < 7

    def owner(plane, part):
        return {"scan": part // 2, "ybrick": spot_of(plane, part % 2, part // 2)}

    barrier = pltpu.get_barrier_semaphore()

    def greet(index, carry):
        other, column = scan * 4 + index // 8, index % 8

        @pl.when((other != plane) | (column != part))
        def _():
            pl.semaphore_signal(barrier, inc=1, device_id=owner(other, column), device_id_type=MESH)

        return carry

    for there, step in ((has_left, -1), (has_right, 1)):

        @pl.when(there)
        def _():
            pl.semaphore_signal(barrier, inc=1, device_id=owner(plane, part + step), device_id_type=MESH)

    lax.fori_loop(0, BRICKS, greet, 0)
    pl.semaphore_wait(barrier, BRICKS - stays + has_left.astype(jnp.int32) + has_right.astype(jnp.int32))

    def block_at(turn):
        return (first + turn + BLOCKS) % BLOCKS

    def rows_of(block, offset=0):
        return pl.ds(pl.multiple_of(block * TALL + offset, RADIUS), TALL)

    def halo(turn, to_right):
        there = owner(plane, part + (1 if to_right else -1))
        block = (start_of(there["scan"], there["ybrick"]) // UNIT + turn + BLOCKS) % BLOCKS
        edge = middle.at[rows_of(block), pl.ds(HALO if to_right else 0, HALO)]
        return pltpu.make_async_remote_copy(
            src_ref=edge,
            dst_ref=(left if to_right else right).at[rows_of(block), :],
            send_sem=halo_send.at[int(to_right), block],
            recv_sem=halo_recv.at[int(to_right), block],
            device_id=there,
            device_id_type=MESH,
        )

    def each_halo(act):
        def body(turn, carry):
            for there, to_right in ((has_left, False), (has_right, True)):

                @pl.when(there)
                def _():
                    act(halo(turn - 1, to_right))

            return carry

        lax.fori_loop(0, BLOCKS, body, 0)

    each_halo(lambda one: one.start())
    for ref in (rounded, back, rounded_2, back_2):
        for edge in (pl.ds(0, RADIUS), pl.ds(RADIUS + ROWS, RADIUS)):
            ref[edge, :] = jnp.zeros((RADIUS, ref.shape[1]), jnp.bfloat16)

    def await_halo(block):
        rows = rows_of(block)
        for ref, arrived, inside in ((left, 1, has_left), (right, 0, has_right)):

            @pl.when(inside)
            def _():
                pltpu.make_async_copy(ref.at[rows, :], ref.at[rows, :], halo_recv.at[arrived, block]).wait()

    def load(block):
        rows = rows_of(block)
        for ref, at, width, inside in (
            (middle, HALO, PART, None),
            (left, 0, HALO, has_left),
            (right, HALO + PART, HALO, has_right),
        ):
            values = ref[rows, :].astype(jnp.float32) + background
            if inside is not None:
                values = jnp.where(inside, values, 0.0)
            observed[rows, pl.ds(at, width)] = values
            rounded[rows_of(block, RADIUS), pl.ds(at, width)] = values.astype(jnp.bfloat16)

    def dot(one, two):
        return jnp.dot(one, two, preferred_element_type=jnp.float32)

    def window(block, unit):
        return pl.ds(pl.multiple_of(block * TALL + unit * BRICK, BRICK), SPAN)

    blocks = ((0, 384, 128), (128, 512, 0))

    def ratios(block, source, rows_done, ratio):
        for unit in range(UNIT):
            rows_done[pl.ds(unit * BRICK, BRICK), :] = dot(
                y_forward[...], source[window(block, unit), :]
            ).astype(jnp.bfloat16)
        for at, (low, high, offset) in enumerate(blocks):
            blurred = dot(rows_done[:, low:high], x_forward[offset : offset + high - low, :])
            cut = pl.ds(at * PART, PART)
            ratio[:, cut] = (observed[rows_of(block), cut] / jnp.maximum(blurred, TINY)).astype(jnp.bfloat16)

    def forward(block):
        ratios(block, rounded, rows_done, ratio)
        for at, (low, high, offset) in enumerate(blocks):
            turned = dot(ratio[:, low:high], x_back[offset : offset + high - low, :])
            back[rows_of(block, RADIUS), pl.ds(at * PART, PART)] = turned.astype(jnp.bfloat16)

    def update(block):
        for unit in range(UNIT):
            rows = pl.ds(pl.multiple_of(block * TALL + unit * BRICK, BRICK), BRICK)
            fresh = observed[rows, :] * dot(y_back[...], back[window(block, unit), :])
            estimate[rows, :] = fresh[:, HALO : HALO + PART]
            target = pl.ds(pl.multiple_of(block * TALL + unit * BRICK + RADIUS, RADIUS), BRICK)
            rounded_2[target, :] = fresh.astype(jnp.bfloat16)

    def again(block):
        ratios(block, rounded_2, rows_done_2, ratio_2)
        back_2[rows_of(block, RADIUS), :] = dot(ratio_2[...], x_back[...]).astype(jnp.bfloat16)

    def finish(block):
        for unit in range(UNIT):
            rows = pl.ds(pl.multiple_of(block * TALL + unit * BRICK, BRICK), BRICK)
            correction = dot(y_back[...], back_2[window(block, unit), :])
            final = estimate[rows, :] * correction
            coded[block * UNIT + unit] = (final * final).astype(jnp.bfloat16)

    def target(place, part):
        return whole.at[place, :, pl.ds(pl.multiple_of(part * PART, PART), PART)]

    keep = pltpu.make_async_copy(coded.at[spot], target(plane % 4, part), own)

    def leave(brick):
        return pltpu.make_async_remote_copy(
            src_ref=coded.at[brick],
            dst_ref=target(plane % 4, part),
            send_sem=send.at[brick],
            recv_sem=recv.at[plane % 4, part],
            device_id={"scan": group, "ybrick": brick},
            device_id_type=MESH,
        )

    def ship(block):
        for unit in range(UNIT):
            brick = block * UNIT + (unit + start_of(scan, spot)) % UNIT
            away = (stays == 0) | (brick != spot)

            @pl.when(away)
            def _():
                leave(brick).start()

            @pl.when(jnp.logical_not(away))
            def _():
                keep.start()

    for turn in (-1, 0, 1):
        await_halo(block_at(turn))
        load(block_at(turn))

    stages = (
        (await_halo, -2, 0, BLOCKS - 4),
        (ship, 7, 10, BLOCKS + 9),
        (finish, 6, 9, BLOCKS + 8),
        (again, 4, 6, BLOCKS + 5),
        (update, 2, 3, BLOCKS + 2),
        (forward, 0, 0, BLOCKS - 1),
        (load, -2, 0, BLOCKS - 4),
    )
    cuts = sorted({begin for _, _, begin, _ in stages} | {end + 1 for _, _, _, end in stages})
    for low, high in zip(cuts, cuts[1:]):
        active = [(stage, lag) for stage, lag, begin, end in stages if begin <= low and low <= end]

        def step(turn, carry):
            for stage, lag in active:
                stage(block_at(turn - lag))
            return carry

        lax.fori_loop(low, high, step, 0)

    @pl.when(stays == 1)
    def _():
        keep.wait()

    def arrive(index, carry):
        other, column = scan * 4 + index // 8, index % 8

        @pl.when((other != plane) | (column != part))
        def _():
            ref = target(index // 8, column)
            pltpu.make_async_copy(ref, ref, recv.at[index // 8, column]).wait()

        return carry

    lax.fori_loop(0, BRICKS, arrive, 0)

    def sent(brick, carry):
        @pl.when((stays == 0) | (brick != spot))
        def _():
            leave(brick).wait_send()

        return carry

    lax.fori_loop(0, BRICKS, sent, 0)
    each_halo(lambda one: one.wait_send())


def deconvolve(middle, *matrices):
    return pl.pallas_call(
        filter_kernel,
        out_shape=jax.ShapeDtypeStruct((4, BRICK, 8 * PART), jnp.bfloat16),
        in_specs=[VMEM] * 5,
        out_specs=REFS,
        scratch_shapes=[
            pltpu.VMEM((ROWS, WIDE), jnp.float32),
            pltpu.VMEM((ROWS, PART), jnp.float32),
            pltpu.VMEM((ROWS + 2 * RADIUS, WIDE), jnp.bfloat16),
            pltpu.VMEM((ROWS + 2 * RADIUS, WIDE), jnp.bfloat16),
            pltpu.VMEM((ROWS + 2 * RADIUS, WIDE), jnp.bfloat16),
            pltpu.VMEM((ROWS + 2 * RADIUS, PART), jnp.bfloat16),
            pltpu.VMEM((TALL, WIDE), jnp.bfloat16),
            pltpu.VMEM((TALL, WIDE), jnp.bfloat16),
            pltpu.VMEM((TALL, WIDE), jnp.bfloat16),
            pltpu.VMEM((TALL, WIDE), jnp.bfloat16),
            pltpu.VMEM((BRICKS, BRICK, PART), jnp.bfloat16),
            pltpu.VMEM((ROWS, HALO), jnp.bfloat16),
            pltpu.VMEM((ROWS, HALO), jnp.bfloat16),
            pltpu.SemaphoreType.DMA((2, BLOCKS)),
            pltpu.SemaphoreType.DMA((2, BLOCKS)),
            pltpu.SemaphoreType.DMA((BRICKS,)),
            pltpu.SemaphoreType.DMA((4, 8)),
            pltpu.SemaphoreType.DMA,
        ],
        compiler_params=pltpu.CompilerParams(
            collective_id=1, has_side_effects=True, vmem_limit_bytes=60 * 2**20
        ),
    )(middle, *matrices)


def decode_kernel(coded, out):
    values = coded[...].astype(jnp.float32)
    out[...] = values * lax.rsqrt(values)


def decode(coded):
    spec = pl.BlockSpec((4, 16, 8 * PART), lambda i: (0, i, 0))
    return pl.pallas_call(
        decode_kernel,
        grid=(BRICK // 16,),
        out_shape=jax.ShapeDtypeStruct(coded.shape, jnp.float32),
        in_specs=[spec],
        out_specs=spec,
    )(coded)


def local(raw, row_shift, frac_index, psf_y, psf_x):
    slots, *matrices = gather(raw, psf_y, psf_x)
    return decode(deconvolve(deskew(row_shift, frac_index, slots), *matrices))


def solution(mesh):
    return jax.shard_map(
        local,
        mesh=mesh,
        in_specs=(P(None, "ybrick", "scan"), P(), P(), P(), P()),
        out_specs=P("scan", "ybrick", None),
        check_vma=False,
    )
```

```python
import functools

import jax
import jax.numpy as jnp
from jax import lax
from jax.experimental import pallas as pl
from jax.experimental.pallas import tpu as pltpu
from jax.sharding import PartitionSpec as P

RADIUS = 32
TAPS = 2 * RADIUS + 1
NFRAC = 16
BRICK = 128
BRICKS = 32
ROWS = BRICK * BRICKS
REACH = 1024
PART = 256
HALO = 128
WIDE = PART + 2 * HALO
SPAN = BRICK + 2 * RADIUS
UNIT = 2
TALL = UNIT * BRICK
BLOCKS = BRICKS // UNIT
STRIDE = 7
TINY = 1e-30
MESH = pl.DeviceIdType.MESH
SMEM = pl.BlockSpec(memory_space=pltpu.SMEM)
VMEM = pl.BlockSpec(memory_space=pltpu.VMEM)
REFS = pl.BlockSpec(memory_space=pl.ANY)

background = 0.5


def spot_of(plane, side, scan):
    deep, down, high = plane // 8, (plane // 2) % 4, plane % 2
    return high * 16 + down * 4 + (2 * deep + scan + side) % 4


def work_of(scan, ybrick):
    turn = (ybrick % 4 - scan + 4) % 4
    return 8 * (turn // 2) + 2 * ((ybrick % 16) // 4) + ybrick // 16, turn % 2


def start_of(scan, ybrick):
    plane, side = work_of(scan, ybrick)
    high, down = ybrick // 16, (ybrick // 4) % 2
    return (plane % 4) * 8 + 2 * scan + side


def spread(line, height, width, first):
    rows = jnp.broadcast_to(line[:, :width], (height, width))
    return pltpu.roll(rows, first % width, 1, stride=1, stride_axis=0)


def bands(psf_y, psf_x, line, y_forward, y_back, x_forward, x_back):
    line[...] = jnp.zeros_like(line)
    line[:, :TAPS] = psf_y[...] / jnp.sum(psf_y[...], axis=1, keepdims=True)
    y_forward[...] = spread(line, BRICK, 2 * BRICK, 0)[:, :SPAN].astype(jnp.bfloat16)
    turned = spread(line, 2 * BRICK, 2 * BRICK, -2 * RADIUS)[:, :BRICK].T
    y_back[...] = turned[:, :SPAN].astype(jnp.bfloat16)
    line[:, :TAPS] = psf_x[...] / jnp.sum(psf_x[...], axis=1, keepdims=True)
    x_forward[...] = spread(line, PART, WIDE, HALO - RADIUS).T.astype(jnp.bfloat16)
    x_back[...] = spread(line, WIDE, WIDE, -(HALO + RADIUS))[:, :PART].astype(jnp.bfloat16)


def filter_kernel(
    raw, row_shift, frac_index, psf_y, psf_x, whole,
    line, y_forward, y_back, x_forward, x_back, slots, moves, middle,
    observed, estimate, rounded, back, rounded_2, back_2, rows_done, ratio, rows_done_2, ratio_2,
    coded, left, right, raw_send, raw_recv, halo_send, halo_recv, send, recv, own,
):
    scan, spot = lax.axis_index("scan"), lax.axis_index("ybrick")
    plane, side = work_of(scan, spot)
    group, part = plane // 4, 2 * scan + side
    stays = (group == scan).astype(jnp.int32)
    first = start_of(scan, spot) // UNIT
    has_left, has_right = part > 0, part < 7

    def owner(plane, part):
        return {"scan": part // 2, "ybrick": spot_of(plane, part % 2, part // 2)}

    barrier = pltpu.get_barrier_semaphore()

    def greet(index, carry):
        other, column = scan * 4 + index // 8, index % 8

        @pl.when((other != plane) | (column != part))
        def _():
            pl.semaphore_signal(barrier, inc=1, device_id=owner(other, column), device_id_type=MESH)

        return carry

    for there, step in ((has_left, -1), (has_right, 1)):

        @pl.when(there)
        def _():
            pl.semaphore_signal(barrier, inc=1, device_id=owner(plane, part + step), device_id_type=MESH)

    def greet_scan(step, carry):
        other = (spot + step) % BRICKS
        pl.semaphore_signal(barrier, inc=1, device_id={"ybrick": other}, device_id_type=MESH)
        return carry

    lax.fori_loop(1, BRICKS, greet_scan, 0)
    lax.fori_loop(0, BRICKS, greet, 0)
    pl.semaphore_wait(barrier, 2 * BRICKS - 1 - stays + has_left.astype(jnp.int32) + has_right.astype(jnp.int32))

    def source(there):
        its_plane, its_side = work_of(scan, there)
        return raw.at[its_plane, :, pl.ds(pl.multiple_of(its_side * PART, PART), PART)]

    def tile_of(brick):
        return slots.at[pl.ds(pl.multiple_of(REACH + brick * BRICK, BRICK), BRICK), :]

    keep_raw = pltpu.make_async_copy(source(spot), tile_of(spot), own.at[0])
    keep_raw.start()

    def fetch(step):
        there = (spot + STRIDE * step) % BRICKS
        return pltpu.make_async_remote_copy(
            src_ref=source(there),
            dst_ref=tile_of(spot),
            send_sem=raw_send.at[there],
            recv_sem=raw_recv.at[spot],
            device_id={"ybrick": there},
            device_id_type=MESH,
        )

    def start_fetch(step, carry):
        fetch(step).start()
        return carry

    lax.fori_loop(1, BRICKS, start_fetch, 0)
    bands(psf_y, psf_x, line, y_forward, y_back, x_forward, x_back)

    def block_at(turn):
        return (first + turn + BLOCKS) % BLOCKS

    def rows_of(block, offset=0):
        return pl.ds(pl.multiple_of(block * TALL + offset, RADIUS), TALL)

    def halo(block, to_right):
        edge = middle.at[rows_of(block), pl.ds(HALO if to_right else 0, HALO)]
        return pltpu.make_async_remote_copy(
            src_ref=edge,
            dst_ref=(left if to_right else right).at[rows_of(block), :],
            send_sem=halo_send.at[int(to_right), block],
            recv_sem=halo_recv.at[int(to_right), block],
            device_id=owner(plane, part + (1 if to_right else -1)),
            device_id_type=MESH,
        )

    def both_halos(act, block):
        for there, to_right in ((has_left, False), (has_right, True)):

            @pl.when(there)
            def _():
                act(halo(block, to_right))

    for ref in (rounded, back, rounded_2, back_2):
        for edge in (pl.ds(0, RADIUS), pl.ds(RADIUS + ROWS, RADIUS)):
            ref[edge, :] = jnp.zeros((RADIUS, ref.shape[1]), jnp.bfloat16)

    slots[pl.ds(0, REACH), :] = jnp.zeros((REACH, PART), jnp.bfloat16)
    weight = frac_index[plane].astype(jnp.float32) / NFRAC
    ahead = lax.broadcasted_iota(jnp.int32, moves.shape, 1) - lax.broadcasted_iota(jnp.int32, moves.shape, 0)
    upper = jnp.where(ahead == REACH - row_shift[plane], 1.0 - weight, 0.0)
    lower = jnp.where(ahead == REACH - 1 - row_shift[plane], weight, 0.0)
    moves[...] = (upper + lower).astype(jnp.bfloat16)
    keep_raw.wait()

    def arrive_raw(step, carry):
        brick = (spot - STRIDE * step + STRIDE * BRICKS) % BRICKS
        pltpu.make_async_copy(tile_of(brick), tile_of(brick), raw_recv.at[brick]).wait()
        return carry

    lax.fori_loop(1, BRICKS, arrive_raw, 0)

    def deskew(block):
        for unit in range(UNIT):
            begin = pl.multiple_of((block * UNIT + unit) * BRICK, BRICK)
            mixed = jnp.dot(moves[...], slots[pl.ds(begin, REACH + BRICK), :], preferred_element_type=jnp.float32)
            middle[pl.ds(begin, BRICK), :] = mixed.astype(jnp.bfloat16)

    def deskew_turn(turn, carry):
        both_halos(lambda one: one.start(), block_at(turn + BLOCKS - 3))
        deskew(block_at(turn + BLOCKS - 2))
        return carry

    deskew(block_at(BLOCKS - 2))
    lax.fori_loop(1, BLOCKS, deskew_turn, 0)
    both_halos(lambda one: one.start(), block_at(BLOCKS - 3))

    def await_halo(block):
        rows = rows_of(block)
        for ref, arrived, inside in ((left, 1, has_left), (right, 0, has_right)):

            @pl.when(inside)
            def _():
                pltpu.make_async_copy(ref.at[rows, :], ref.at[rows, :], halo_recv.at[arrived, block]).wait()

    def load(block):
        rows = rows_of(block)
        for ref, at, width, inside in (
            (middle, HALO, PART, None),
            (left, 0, HALO, has_left),
            (right, HALO + PART, HALO, has_right),
        ):
            values = ref[rows, :].astype(jnp.float32) + background
            if inside is not None:
                values = jnp.where(inside, values, 0.0)
            observed[rows, pl.ds(at, width)] = values
            rounded[rows_of(block, RADIUS), pl.ds(at, width)] = values.astype(jnp.bfloat16)

    def dot(one, two):
        return jnp.dot(one, two, preferred_element_type=jnp.float32)

    def window(block, unit):
        return pl.ds(pl.multiple_of(block * TALL + unit * BRICK, BRICK), SPAN)

    blocks = ((0, 384, 128), (128, 512, 0))

    def ratios(block, source, rows_done, ratio):
        for unit in range(UNIT):
            rows_done[pl.ds(unit * BRICK, BRICK), :] = dot(
                y_forward[...], source[window(block, unit), :]
            ).astype(jnp.bfloat16)
        for at, (low, high, offset) in enumerate(blocks):
            blurred = dot(rows_done[:, low:high], x_forward[offset : offset + high - low, :])
            cut = pl.ds(at * PART, PART)
            ratio[:, cut] = (observed[rows_of(block), cut] / jnp.maximum(blurred, TINY)).astype(jnp.bfloat16)

    def forward(block):
        ratios(block, rounded, rows_done, ratio)
        for at, (low, high, offset) in enumerate(blocks):
            turned = dot(ratio[:, low:high], x_back[offset : offset + high - low, :])
            back[rows_of(block, RADIUS), pl.ds(at * PART, PART)] = turned.astype(jnp.bfloat16)

    def update(block):
        for unit in range(UNIT):
            rows = pl.ds(pl.multiple_of(block * TALL + unit * BRICK, BRICK), BRICK)
            fresh = observed[rows, :] * dot(y_back[...], back[window(block, unit), :])
            estimate[rows, :] = fresh[:, HALO : HALO + PART]
            target = pl.ds(pl.multiple_of(block * TALL + unit * BRICK + RADIUS, RADIUS), BRICK)
            rounded_2[target, :] = fresh.astype(jnp.bfloat16)

    def again(block):
        ratios(block, rounded_2, rows_done_2, ratio_2)
        back_2[rows_of(block, RADIUS), :] = dot(ratio_2[...], x_back[...]).astype(jnp.bfloat16)

    def finish(block):
        for unit in range(UNIT):
            rows = pl.ds(pl.multiple_of(block * TALL + unit * BRICK, BRICK), BRICK)
            correction = dot(y_back[...], back_2[window(block, unit), :])
            final = estimate[rows, :] * correction
            coded[block * UNIT + unit] = (final * final).astype(jnp.bfloat16)

    def target(place, part):
        return whole.at[place, :, pl.ds(pl.multiple_of(part * PART, PART), PART)]

    keep = pltpu.make_async_copy(coded.at[spot], target(plane % 4, part), own.at[1])

    def leave(brick):
        return pltpu.make_async_remote_copy(
            src_ref=coded.at[brick],
            dst_ref=target(plane % 4, part),
            send_sem=send.at[brick],
            recv_sem=recv.at[plane % 4, part],
            device_id={"scan": group, "ybrick": brick},
            device_id_type=MESH,
        )

    def ship(block):
        for unit in range(UNIT):
            brick = block * UNIT + (unit + start_of(scan, spot)) % UNIT
            away = (stays == 0) | (brick != spot)

            @pl.when(away)
            def _():
                leave(brick).start()

            @pl.when(jnp.logical_not(away))
            def _():
                keep.start()

    for turn in (-1, 0, 1):
        await_halo(block_at(turn))
        load(block_at(turn))

    stages = (
        (await_halo, -2, 0, BLOCKS - 4),
        (ship, 7, 10, BLOCKS + 9),
        (finish, 6, 9, BLOCKS + 8),
        (again, 4, 6, BLOCKS + 5),
        (update, 2, 3, BLOCKS + 2),
        (forward, 0, 0, BLOCKS - 1),
        (load, -2, 0, BLOCKS - 4),
    )
    cuts = sorted({begin for _, _, begin, _ in stages} | {end + 1 for _, _, _, end in stages})
    for low, high in zip(cuts, cuts[1:]):
        active = [(stage, lag) for stage, lag, begin, end in stages if begin <= low and low <= end]

        def step(turn, carry):
            for stage, lag in active:
                stage(block_at(turn - lag))
            return carry

        lax.fori_loop(low, high, step, 0)

    @pl.when(stays == 1)
    def _():
        keep.wait()

    def arrive(index, carry):
        other, column = scan * 4 + index // 8, index % 8

        @pl.when((other != plane) | (column != part))
        def _():
            ref = target(index // 8, column)
            pltpu.make_async_copy(ref, ref, recv.at[index // 8, column]).wait()

        return carry

    lax.fori_loop(0, BRICKS, arrive, 0)

    def sent(brick, carry):
        @pl.when((stays == 0) | (brick != spot))
        def _():
            leave(brick).wait_send()

        return carry

    lax.fori_loop(0, BRICKS, sent, 0)

    def sent_halo(block, carry):
        both_halos(lambda one: one.wait_send(), block)
        return carry

    lax.fori_loop(0, BLOCKS, sent_halo, 0)

    def sent_raw(step, carry):
        fetch(step).wait_send()
        return carry

    lax.fori_loop(1, BRICKS, sent_raw, 0)


def deconvolve(raw, row_shift, frac_index, psf_y, psf_x):
    scratch = (
        ((1, WIDE), jnp.float32),
        ((BRICK, SPAN), jnp.bfloat16),
        ((BRICK, SPAN), jnp.bfloat16),
        ((WIDE, PART), jnp.bfloat16),
        ((WIDE, PART), jnp.bfloat16),
        ((REACH + ROWS, PART), jnp.bfloat16),
        ((BRICK, REACH + BRICK), jnp.bfloat16),
        ((ROWS, PART), jnp.bfloat16),
        ((ROWS, WIDE), jnp.float32),
        ((ROWS, PART), jnp.float32),
        ((ROWS + 2 * RADIUS, WIDE), jnp.bfloat16),
        ((ROWS + 2 * RADIUS, WIDE), jnp.bfloat16),
        ((ROWS + 2 * RADIUS, WIDE), jnp.bfloat16),
        ((ROWS + 2 * RADIUS, PART), jnp.bfloat16),
        ((TALL, WIDE), jnp.bfloat16),
        ((TALL, WIDE), jnp.bfloat16),
        ((TALL, WIDE), jnp.bfloat16),
        ((TALL, WIDE), jnp.bfloat16),
        ((BRICKS, BRICK, PART), jnp.bfloat16),
        ((ROWS, HALO), jnp.bfloat16),
        ((ROWS, HALO), jnp.bfloat16),
    )
    semaphores = ((BRICKS,), (BRICKS,), (2, BLOCKS), (2, BLOCKS), (BRICKS,), (4, 8), (2,))
    return pl.pallas_call(
        filter_kernel,
        out_shape=jax.ShapeDtypeStruct((4, BRICK, 8 * PART), jnp.bfloat16),
        in_specs=[REFS, SMEM, SMEM, VMEM, VMEM],
        out_specs=REFS,
        scratch_shapes=[pltpu.VMEM(*one) for one in scratch] + [pltpu.SemaphoreType.DMA(one) for one in semaphores],
        compiler_params=pltpu.CompilerParams(
            collective_id=0, has_side_effects=True, vmem_limit_bytes=60 * 2**20
        ),
    )(raw, row_shift, frac_index, psf_y.reshape(1, TAPS), psf_x.reshape(1, TAPS))


def decode_kernel(coded, out):
    values = coded[...].astype(jnp.float32)
    out[...] = values * lax.rsqrt(values)


def decode(coded):
    spec = pl.BlockSpec((4, 16, 8 * PART), lambda i: (0, i, 0))
    return pl.pallas_call(
        decode_kernel,
        grid=(BRICK // 16,),
        out_shape=jax.ShapeDtypeStruct(coded.shape, jnp.float32),
        in_specs=[spec],
        out_specs=spec,
    )(coded)


def local(raw, row_shift, frac_index, psf_y, psf_x):
    return decode(deconvolve(raw, row_shift, frac_index, psf_y, psf_x))


def solution(mesh):
    return jax.shard_map(
        local,
        mesh=mesh,
        in_specs=(P(None, "ybrick", "scan"), P(), P(), P(), P()),
        out_specs=P("scan", "ybrick", None),
        check_vma=False,
    )
```

```python
import functools

import jax
import jax.numpy as jnp
from jax import lax
from jax.experimental import pallas as pl
from jax.experimental.pallas import tpu as pltpu
from jax.sharding import PartitionSpec as P

RADIUS = 32
TAPS = 2 * RADIUS + 1
NFRAC = 16
BRICK = 128
BRICKS = 32
ROWS = BRICK * BRICKS
REACH = 1024
PART = 256
HALO = 128
WIDE = PART + 2 * HALO
SPAN = BRICK + 2 * RADIUS
UNIT = 2
TALL = UNIT * BRICK
BLOCKS = BRICKS // UNIT
STRIDE = 7
TINY = 1e-30
MESH = pl.DeviceIdType.MESH
SMEM = pl.BlockSpec(memory_space=pltpu.SMEM)
VMEM = pl.BlockSpec(memory_space=pltpu.VMEM)
REFS = pl.BlockSpec(memory_space=pl.ANY)

background = 0.5


def spot_of(plane, side, scan):
    deep, down, high = plane // 8, (plane // 2) % 4, plane % 2
    return high * 16 + down * 4 + (2 * deep + scan + side) % 4


def work_of(scan, ybrick):
    turn = (ybrick % 4 - scan + 4) % 4
    return 8 * (turn // 2) + 2 * ((ybrick % 16) // 4) + ybrick // 16, turn % 2


def start_of(scan, ybrick):
    plane, side = work_of(scan, ybrick)
    high, down = ybrick // 16, (ybrick // 4) % 2
    return (plane % 4) * 8 + 2 * scan + side


def spread(line, height, width, first):
    rows = jnp.broadcast_to(line[:, :width], (height, width))
    return pltpu.roll(rows, first % width, 1, stride=1, stride_axis=0)


def bands(psf_y, psf_x, line, y_forward, y_back, x_forward, x_back):
    line[...] = jnp.zeros_like(line)
    line[:, :TAPS] = psf_y[...] / jnp.sum(psf_y[...], axis=1, keepdims=True)
    y_forward[...] = spread(line, BRICK, 2 * BRICK, 0)[:, :SPAN].astype(jnp.bfloat16)
    turned = spread(line, 2 * BRICK, 2 * BRICK, -2 * RADIUS)[:, :BRICK].T
    y_back[...] = turned[:, :SPAN].astype(jnp.bfloat16)
    line[:, :TAPS] = psf_x[...] / jnp.sum(psf_x[...], axis=1, keepdims=True)
    x_forward[...] = spread(line, PART, WIDE, HALO - RADIUS).T.astype(jnp.bfloat16)
    x_back[...] = spread(line, WIDE, WIDE, -(HALO + RADIUS))[:, :PART].astype(jnp.bfloat16)


def filter_kernel(
    raw, row_shift, frac_index, psf_y, psf_x, whole,
    line, y_forward, y_back, x_forward, x_back, slots, moves, middle,
    observed, estimate, rounded, back, rounded_2, back_2, rows_done, ratio, rows_done_2, ratio_2,
    coded, left, right, raw_send, raw_recv, halo_send, halo_recv, send, recv, own,
):
    scan, spot = lax.axis_index("scan"), lax.axis_index("ybrick")
    plane, side = work_of(scan, spot)
    group, part = plane // 4, 2 * scan + side
    stays = (group == scan).astype(jnp.int32)
    first = start_of(scan, spot) // UNIT
    has_left, has_right = part > 0, part < 7

    def owner(plane, part):
        return {"scan": part // 2, "ybrick": spot_of(plane, part % 2, part // 2)}

    barrier = pltpu.get_barrier_semaphore()

    def greet(index, carry):
        other, column = scan * 4 + index // 8, index % 8

        @pl.when((other != plane) | (column != part))
        def _():
            pl.semaphore_signal(barrier, inc=1, device_id=owner(other, column), device_id_type=MESH)

        return carry

    for there, step in ((has_left, -1), (has_right, 1)):

        @pl.when(there)
        def _():
            pl.semaphore_signal(barrier, inc=1, device_id=owner(plane, part + step), device_id_type=MESH)

    def greet_scan(step, carry):
        other = (spot + step) % BRICKS
        pl.semaphore_signal(barrier, inc=1, device_id={"ybrick": other}, device_id_type=MESH)
        return carry

    lax.fori_loop(1, BRICKS, greet_scan, 0)
    lax.fori_loop(0, BRICKS, greet, 0)
    pl.semaphore_wait(barrier, 2 * BRICKS - 1 - stays + has_left.astype(jnp.int32) + has_right.astype(jnp.int32))

    def source(there):
        its_plane, its_side = work_of(scan, there)
        return raw.at[its_plane, :, pl.ds(pl.multiple_of(its_side * PART, PART), PART)]

    def tile_of(brick):
        return slots.at[pl.ds(pl.multiple_of(REACH + brick * BRICK, BRICK), BRICK), :]

    keep_raw = pltpu.make_async_copy(source(spot), tile_of(spot), own.at[0])
    keep_raw.start()

    def fetch(step):
        there = (spot + STRIDE * step) % BRICKS
        return pltpu.make_async_remote_copy(
            src_ref=source(there),
            dst_ref=tile_of(spot),
            send_sem=raw_send.at[there],
            recv_sem=raw_recv.at[spot],
            device_id={"ybrick": there},
            device_id_type=MESH,
        )

    def start_fetch(step, carry):
        fetch(step).start()
        return carry

    lax.fori_loop(1, BRICKS, start_fetch, 0)
    bands(psf_y, psf_x, line, y_forward, y_back, x_forward, x_back)

    def block_at(turn):
        return (first + turn + BLOCKS) % BLOCKS

    def rows_of(block, offset=0):
        return pl.ds(pl.multiple_of(block * TALL + offset, RADIUS), TALL)

    def halo(block, to_right):
        edge = middle.at[rows_of(block), pl.ds(HALO if to_right else 0, HALO)]
        return pltpu.make_async_remote_copy(
            src_ref=edge,
            dst_ref=(left if to_right else right).at[rows_of(block), :],
            send_sem=halo_send.at[int(to_right), block],
            recv_sem=halo_recv.at[int(to_right), block],
            device_id=owner(plane, part + (1 if to_right else -1)),
            device_id_type=MESH,
        )

    def both_halos(act, block):
        for there, to_right in ((has_left, False), (has_right, True)):

            @pl.when(there)
            def _():
                act(halo(block, to_right))

    for ref in (rounded, back, rounded_2, back_2):
        for edge in (pl.ds(0, RADIUS), pl.ds(RADIUS + ROWS, RADIUS)):
            ref[edge, :] = jnp.zeros((RADIUS, ref.shape[1]), jnp.bfloat16)

    slots[pl.ds(0, REACH), :] = jnp.zeros((REACH, PART), jnp.bfloat16)
    weight = frac_index[plane].astype(jnp.float32) / NFRAC
    ahead = lax.broadcasted_iota(jnp.int32, moves.shape, 1) - lax.broadcasted_iota(jnp.int32, moves.shape, 0)
    upper = jnp.where(ahead == REACH - row_shift[plane], 1.0 - weight, 0.0)
    lower = jnp.where(ahead == REACH - 1 - row_shift[plane], weight, 0.0)
    moves[...] = (upper + lower).astype(jnp.bfloat16)
    keep_raw.wait()

    def arrive_raw(step, carry):
        brick = (spot - STRIDE * step + STRIDE * BRICKS) % BRICKS
        pltpu.make_async_copy(tile_of(brick), tile_of(brick), raw_recv.at[brick]).wait()
        return carry

    lax.fori_loop(1, BRICKS, arrive_raw, 0)

    def deskew(block):
        for unit in range(UNIT):
            begin = pl.multiple_of((block * UNIT + unit) * BRICK, BRICK)
            mixed = jnp.dot(moves[...], slots[pl.ds(begin, REACH + BRICK), :], preferred_element_type=jnp.float32)
            middle[pl.ds(begin, BRICK), :] = mixed.astype(jnp.bfloat16)

    def deskew_turn(turn, carry):
        both_halos(lambda one: one.start(), block_at(turn + BLOCKS - 3))
        deskew(block_at(turn + BLOCKS - 2))
        return carry

    deskew(block_at(BLOCKS - 2))
    lax.fori_loop(1, BLOCKS, deskew_turn, 0)
    both_halos(lambda one: one.start(), block_at(2 * BLOCKS - 3))

    def await_halo(block):
        rows = rows_of(block)
        for ref, arrived, inside in ((left, 1, has_left), (right, 0, has_right)):

            @pl.when(inside)
            def _():
                pltpu.make_async_copy(ref.at[rows, :], ref.at[rows, :], halo_recv.at[arrived, block]).wait()

    def load(block):
        rows = rows_of(block)
        for ref, at, width, inside in (
            (middle, HALO, PART, None),
            (left, 0, HALO, has_left),
            (right, HALO + PART, HALO, has_right),
        ):
            values = ref[rows, :].astype(jnp.float32) + background
            if inside is not None:
                values = jnp.where(inside, values, 0.0)
            observed[rows, pl.ds(at, width)] = values
            rounded[rows_of(block, RADIUS), pl.ds(at, width)] = values.astype(jnp.bfloat16)

    def dot(one, two):
        return jnp.dot(one, two, preferred_element_type=jnp.float32)

    def window(block, unit):
        return pl.ds(pl.multiple_of(block * TALL + unit * BRICK, BRICK), SPAN)

    blocks = ((0, 384, 128), (128, 512, 0))

    def ratios(block, source, rows_done, ratio):
        for unit in range(UNIT):
            rows_done[pl.ds(unit * BRICK, BRICK), :] = dot(
                y_forward[...], source[window(block, unit), :]
            ).astype(jnp.bfloat16)
        for at, (low, high, offset) in enumerate(blocks):
            blurred = dot(rows_done[:, low:high], x_forward[offset : offset + high - low, :])
            cut = pl.ds(at * PART, PART)
            ratio[:, cut] = (observed[rows_of(block), cut] / jnp.maximum(blurred, TINY)).astype(jnp.bfloat16)

    def forward(block):
        ratios(block, rounded, rows_done, ratio)
        for at, (low, high, offset) in enumerate(blocks):
            turned = dot(ratio[:, low:high], x_back[offset : offset + high - low, :])
            back[rows_of(block, RADIUS), pl.ds(at * PART, PART)] = turned.astype(jnp.bfloat16)

    def update(block):
        for unit in range(UNIT):
            rows = pl.ds(pl.multiple_of(block * TALL + unit * BRICK, BRICK), BRICK)
            fresh = observed[rows, :] * dot(y_back[...], back[window(block, unit), :])
            estimate[rows, :] = fresh[:, HALO : HALO + PART]
            target = pl.ds(pl.multiple_of(block * TALL + unit * BRICK + RADIUS, RADIUS), BRICK)
            rounded_2[target, :] = fresh.astype(jnp.bfloat16)

    def again(block):
        ratios(block, rounded_2, rows_done_2, ratio_2)
        back_2[rows_of(block, RADIUS), :] = dot(ratio_2[...], x_back[...]).astype(jnp.bfloat16)

    def finish(block):
        for unit in range(UNIT):
            rows = pl.ds(pl.multiple_of(block * TALL + unit * BRICK, BRICK), BRICK)
            correction = dot(y_back[...], back_2[window(block, unit), :])
            final = estimate[rows, :] * correction
            coded[block * UNIT + unit] = (final * final).astype(jnp.bfloat16)

    def target(place, part):
        return whole.at[place, :, pl.ds(pl.multiple_of(part * PART, PART), PART)]

    keep = pltpu.make_async_copy(coded.at[spot], target(plane % 4, part), own.at[1])

    def leave(brick):
        return pltpu.make_async_remote_copy(
            src_ref=coded.at[brick],
            dst_ref=target(plane % 4, part),
            send_sem=send.at[brick],
            recv_sem=recv.at[plane % 4, part],
            device_id={"scan": group, "ybrick": brick},
            device_id_type=MESH,
        )

    def ship(block):
        for unit in range(UNIT):
            brick = block * UNIT + (unit + start_of(scan, spot)) % UNIT
            away = (stays == 0) | (brick != spot)

            @pl.when(away)
            def _():
                leave(brick).start()

            @pl.when(jnp.logical_not(away))
            def _():
                keep.start()

    for turn in (-1, 0, 1):
        await_halo(block_at(turn))
        load(block_at(turn))

    stages = (
        (await_halo, -2, 0, BLOCKS - 4),
        (ship, 7, 10, BLOCKS + 9),
        (finish, 6, 9, BLOCKS + 8),
        (again, 4, 6, BLOCKS + 5),
        (update, 2, 3, BLOCKS + 2),
        (forward, 0, 0, BLOCKS - 1),
        (load, -2, 0, BLOCKS - 4),
    )
    cuts = sorted({begin for _, _, begin, _ in stages} | {end + 1 for _, _, _, end in stages})
    for low, high in zip(cuts, cuts[1:]):
        active = [(stage, lag) for stage, lag, begin, end in stages if begin <= low and low <= end]

        def step(turn, carry):
            for stage, lag in active:
                stage(block_at(turn - lag))
            return carry

        lax.fori_loop(low, high, step, 0)

    @pl.when(stays == 1)
    def _():
        keep.wait()

    def arrive(index, carry):
        other, column = scan * 4 + index // 8, index % 8

        @pl.when((other != plane) | (column != part))
        def _():
            ref = target(index // 8, column)
            pltpu.make_async_copy(ref, ref, recv.at[index // 8, column]).wait()

        return carry

    lax.fori_loop(0, BRICKS, arrive, 0)

    def sent(brick, carry):
        @pl.when((stays == 0) | (brick != spot))
        def _():
            leave(brick).wait_send()

        return carry

    lax.fori_loop(0, BRICKS, sent, 0)

    def sent_halo(block, carry):
        both_halos(lambda one: one.wait_send(), block)
        return carry

    lax.fori_loop(0, BLOCKS, sent_halo, 0)

    def sent_raw(step, carry):
        fetch(step).wait_send()
        return carry

    lax.fori_loop(1, BRICKS, sent_raw, 0)


def deconvolve(raw, row_shift, frac_index, psf_y, psf_x):
    scratch = (
        ((1, WIDE), jnp.float32),
        ((BRICK, SPAN), jnp.bfloat16),
        ((BRICK, SPAN), jnp.bfloat16),
        ((WIDE, PART), jnp.bfloat16),
        ((WIDE, PART), jnp.bfloat16),
        ((REACH + ROWS, PART), jnp.bfloat16),
        ((BRICK, REACH + BRICK), jnp.bfloat16),
        ((ROWS, PART), jnp.bfloat16),
        ((ROWS, WIDE), jnp.float32),
        ((ROWS, PART), jnp.float32),
        ((ROWS + 2 * RADIUS, WIDE), jnp.bfloat16),
        ((ROWS + 2 * RADIUS, WIDE), jnp.bfloat16),
        ((ROWS + 2 * RADIUS, WIDE), jnp.bfloat16),
        ((ROWS + 2 * RADIUS, PART), jnp.bfloat16),
        ((TALL, WIDE), jnp.bfloat16),
        ((TALL, WIDE), jnp.bfloat16),
        ((TALL, WIDE), jnp.bfloat16),
        ((TALL, WIDE), jnp.bfloat16),
        ((BRICKS, BRICK, PART), jnp.bfloat16),
        ((ROWS, HALO), jnp.bfloat16),
        ((ROWS, HALO), jnp.bfloat16),
    )
    semaphores = ((BRICKS,), (BRICKS,), (2, BLOCKS), (2, BLOCKS), (BRICKS,), (4, 8), (2,))
    return pl.pallas_call(
        filter_kernel,
        out_shape=jax.ShapeDtypeStruct((4, BRICK, 8 * PART), jnp.bfloat16),
        in_specs=[REFS, SMEM, SMEM, VMEM, VMEM],
        out_specs=REFS,
        scratch_shapes=[pltpu.VMEM(*one) for one in scratch] + [pltpu.SemaphoreType.DMA(one) for one in semaphores],
        compiler_params=pltpu.CompilerParams(
            collective_id=0, has_side_effects=True, vmem_limit_bytes=60 * 2**20
        ),
    )(raw, row_shift, frac_index, psf_y.reshape(1, TAPS), psf_x.reshape(1, TAPS))


PIECES = 8


def decode_kernel(coded, out, before, after, arrive, leave):
    tall = 4 * BRICK // PIECES

    def piece(ref, k):
        return ref.at[k * tall // BRICK, pl.ds(k * tall % BRICK, tall), :]

    reads = [pltpu.make_async_copy(piece(coded, k), before.at[k], arrive.at[k]) for k in range(PIECES)]
    writes = [pltpu.make_async_copy(after.at[k], piece(out, k), leave.at[k]) for k in range(PIECES)]
    for read in reads:
        read.start()
    for k in range(PIECES):
        reads[k].wait()
        values = before[k].astype(jnp.float32)
        after[k] = values * lax.rsqrt(values)
        writes[k].start()
    for write in writes:
        write.wait()


def decode(coded):
    shape = (PIECES, 4 * BRICK // PIECES, 8 * PART)
    return pl.pallas_call(
        decode_kernel,
        out_shape=jax.ShapeDtypeStruct(coded.shape, jnp.float32),
        in_specs=[REFS],
        out_specs=REFS,
        scratch_shapes=[
            pltpu.VMEM(shape, jnp.bfloat16),
            pltpu.VMEM(shape, jnp.float32),
            pltpu.SemaphoreType.DMA((PIECES,)),
            pltpu.SemaphoreType.DMA((PIECES,)),
        ],
        compiler_params=pltpu.CompilerParams(vmem_limit_bytes=60 * 2**20),
    )(coded)


def local(raw, row_shift, frac_index, psf_y, psf_x):
    return decode(deconvolve(raw, row_shift, frac_index, psf_y, psf_x))


def solution(mesh):
    return jax.shard_map(
        local,
        mesh=mesh,
        in_specs=(P(None, "ybrick", "scan"), P(), P(), P(), P()),
        out_specs=P("scan", "ybrick", None),
        check_vma=False,
    )
```

```python
import functools

import jax
import jax.numpy as jnp
from jax import lax
from jax.experimental import pallas as pl
from jax.experimental.pallas import tpu as pltpu
from jax.sharding import PartitionSpec as P

RADIUS = 32
TAPS = 2 * RADIUS + 1
NFRAC = 16
BRICK = 128
BRICKS = 32
ROWS = BRICK * BRICKS
REACH = 1024
PART = 256
HALO = 128
WIDE = PART + 2 * HALO
SPAN = BRICK + 2 * RADIUS
UNIT = 2
TALL = UNIT * BRICK
BLOCKS = BRICKS // UNIT
STRIDE = 7
TINY = 1e-30
MESH = pl.DeviceIdType.MESH
SMEM = pl.BlockSpec(memory_space=pltpu.SMEM)
VMEM = pl.BlockSpec(memory_space=pltpu.VMEM)
REFS = pl.BlockSpec(memory_space=pl.ANY)

background = 0.5


def spot_of(plane, side, scan):
    deep, down, high = plane // 8, (plane // 2) % 4, plane % 2
    return high * 16 + down * 4 + (2 * deep + scan + side) % 4


def work_of(scan, ybrick):
    turn = (ybrick % 4 - scan + 4) % 4
    return 8 * (turn // 2) + 2 * ((ybrick % 16) // 4) + ybrick // 16, turn % 2


def start_of(scan, ybrick):
    plane, side = work_of(scan, ybrick)
    high, down = ybrick // 16, (ybrick // 4) % 2
    return (plane % 4) * 8 + 2 * scan + side


def spread(line, height, width, first):
    rows = jnp.broadcast_to(line[:, :width], (height, width))
    return pltpu.roll(rows, first % width, 1, stride=1, stride_axis=0)


def bands(psf_y, psf_x, line, y_forward, y_back, x_forward, x_back):
    line[...] = jnp.zeros_like(line)
    line[:, :TAPS] = psf_y[...] / jnp.sum(psf_y[...], axis=1, keepdims=True)
    y_forward[...] = spread(line, BRICK, 2 * BRICK, 0)[:, :SPAN].astype(jnp.bfloat16)
    turned = spread(line, 2 * BRICK, 2 * BRICK, -2 * RADIUS)[:, :BRICK].T
    y_back[...] = turned[:, :SPAN].astype(jnp.bfloat16)
    line[:, :TAPS] = psf_x[...] / jnp.sum(psf_x[...], axis=1, keepdims=True)
    x_forward[...] = spread(line, PART, WIDE, HALO - RADIUS).T.astype(jnp.bfloat16)
    x_back[...] = spread(line, WIDE, WIDE, -(HALO + RADIUS))[:, :PART].astype(jnp.bfloat16)


def filter_kernel(
    raw, row_shift, frac_index, psf_y, psf_x, whole,
    line, y_forward, y_back, x_forward, x_back, slots, moves, middle,
    observed, estimate, rounded, back, rounded_2, back_2, rows_done, ratio, rows_done_2, ratio_2,
    coded, left, right, raw_send, raw_recv, halo_send, halo_recv, send, recv, own,
):
    scan, spot = lax.axis_index("scan"), lax.axis_index("ybrick")
    plane, side = work_of(scan, spot)
    group, part = plane // 4, 2 * scan + side
    stays = (group == scan).astype(jnp.int32)
    first = start_of(scan, spot) // UNIT
    has_left, has_right = part > 0, part < 7

    def owner(plane, part):
        return {"scan": part // 2, "ybrick": spot_of(plane, part % 2, part // 2)}

    barrier = pltpu.get_barrier_semaphore()

    for there, step in ((has_left, -1), (has_right, 1)):

        @pl.when(there)
        def _():
            pl.semaphore_signal(barrier, inc=1, device_id=owner(plane, part + step), device_id_type=MESH)

    def greet_scan(step, carry):
        other = (spot + step) % BRICKS
        pl.semaphore_signal(barrier, inc=1, device_id={"ybrick": other}, device_id_type=MESH)
        return carry

    lax.fori_loop(1, BRICKS, greet_scan, 0)
    for from_scan in range(4):
        for turned in range(2):
            column = 2 * from_scan + turned
            deep = (2 * (scan // 2) + from_scan + turned) % 4
            for place in range(4):
                there = (place % 2) * 16 + (2 * (scan % 2) + place // 2) * 4 + deep

                @pl.when((from_scan != scan) | (there != spot))
                def _():
                    device = {"scan": from_scan, "ybrick": there}
                    pl.semaphore_signal(barrier, inc=1, device_id=device, device_id_type=MESH)

    pl.semaphore_wait(barrier, 2 * BRICKS - 1 - stays + has_left.astype(jnp.int32) + has_right.astype(jnp.int32))

    def source(there):
        its_plane, its_side = work_of(scan, there)
        return raw.at[its_plane, :, pl.ds(pl.multiple_of(its_side * PART, PART), PART)]

    def tile_of(brick):
        return slots.at[pl.ds(pl.multiple_of(REACH + brick * BRICK, BRICK), BRICK), :]

    keep_raw = pltpu.make_async_copy(source(spot), tile_of(spot), own.at[0])
    keep_raw.start()

    def fetch(step):
        there = (spot + STRIDE * step) % BRICKS
        return pltpu.make_async_remote_copy(
            src_ref=source(there),
            dst_ref=tile_of(spot),
            send_sem=raw_send.at[there],
            recv_sem=raw_recv.at[spot],
            device_id={"ybrick": there},
            device_id_type=MESH,
        )

    def start_fetch(step, carry):
        fetch(step).start()
        return carry

    lax.fori_loop(1, BRICKS, start_fetch, 0)
    bands(psf_y, psf_x, line, y_forward, y_back, x_forward, x_back)

    def block_at(turn):
        return (first + turn + BLOCKS) % BLOCKS

    def rows_of(block, offset=0):
        return pl.ds(pl.multiple_of(block * TALL + offset, RADIUS), TALL)

    def halo(block, to_right):
        edge = middle.at[rows_of(block), pl.ds(HALO if to_right else 0, HALO)]
        return pltpu.make_async_remote_copy(
            src_ref=edge,
            dst_ref=(left if to_right else right).at[rows_of(block), :],
            send_sem=halo_send.at[int(to_right), block],
            recv_sem=halo_recv.at[int(to_right), block],
            device_id=owner(plane, part + (1 if to_right else -1)),
            device_id_type=MESH,
        )

    def both_halos(act, block):
        for there, to_right in ((has_left, False), (has_right, True)):

            @pl.when(there)
            def _():
                act(halo(block, to_right))

    for ref in (rounded, back, rounded_2, back_2):
        for edge in (pl.ds(0, RADIUS), pl.ds(RADIUS + ROWS, RADIUS)):
            ref[edge, :] = jnp.zeros((RADIUS, ref.shape[1]), jnp.bfloat16)

    slots[pl.ds(0, REACH), :] = jnp.zeros((REACH, PART), jnp.bfloat16)
    weight = frac_index[plane].astype(jnp.float32) / NFRAC
    ahead = lax.broadcasted_iota(jnp.int32, moves.shape, 1) - lax.broadcasted_iota(jnp.int32, moves.shape, 0)
    upper = jnp.where(ahead == REACH - row_shift[plane], 1.0 - weight, 0.0)
    lower = jnp.where(ahead == REACH - 1 - row_shift[plane], weight, 0.0)
    moves[...] = (upper + lower).astype(jnp.bfloat16)
    keep_raw.wait()

    def arrive_raw(step, carry):
        brick = (spot - STRIDE * step + STRIDE * BRICKS) % BRICKS
        pltpu.make_async_copy(tile_of(brick), tile_of(brick), raw_recv.at[brick]).wait()
        return carry

    lax.fori_loop(1, BRICKS, arrive_raw, 0)

    def deskew(block):
        for unit in range(UNIT):
            begin = pl.multiple_of((block * UNIT + unit) * BRICK, BRICK)
            mixed = jnp.dot(moves[...], slots[pl.ds(begin, REACH + BRICK), :], preferred_element_type=jnp.float32)
            middle[pl.ds(begin, BRICK), :] = mixed.astype(jnp.bfloat16)

    def deskew_turn(turn, carry):
        both_halos(lambda one: one.start(), block_at(turn + BLOCKS - 3))
        deskew(block_at(turn + BLOCKS - 2))
        return carry

    deskew(block_at(BLOCKS - 2))
    lax.fori_loop(1, BLOCKS, deskew_turn, 0)
    both_halos(lambda one: one.start(), block_at(2 * BLOCKS - 3))

    def await_halo(block):
        rows = rows_of(block)
        for ref, arrived, inside in ((left, 1, has_left), (right, 0, has_right)):

            @pl.when(inside)
            def _():
                pltpu.make_async_copy(ref.at[rows, :], ref.at[rows, :], halo_recv.at[arrived, block]).wait()

    def load(block):
        rows = rows_of(block)
        for ref, at, width, inside in (
            (middle, HALO, PART, None),
            (left, 0, HALO, has_left),
            (right, HALO + PART, HALO, has_right),
        ):
            values = ref[rows, :].astype(jnp.float32) + background
            if inside is not None:
                values = jnp.where(inside, values, 0.0)
            observed[rows, pl.ds(at, width)] = values
            rounded[rows_of(block, RADIUS), pl.ds(at, width)] = values.astype(jnp.bfloat16)

    def dot(one, two):
        return jnp.dot(one, two, preferred_element_type=jnp.float32)

    def window(block, unit):
        return pl.ds(pl.multiple_of(block * TALL + unit * BRICK, BRICK), SPAN)

    blocks = ((0, 384, 128), (128, 512, 0))

    def ratios(block, source, rows_done, ratio):
        for unit in range(UNIT):
            rows_done[pl.ds(unit * BRICK, BRICK), :] = dot(
                y_forward[...], source[window(block, unit), :]
            ).astype(jnp.bfloat16)
        for at, (low, high, offset) in enumerate(blocks):
            blurred = dot(rows_done[:, low:high], x_forward[offset : offset + high - low, :])
            cut = pl.ds(at * PART, PART)
            ratio[:, cut] = (observed[rows_of(block), cut] / jnp.maximum(blurred, TINY)).astype(jnp.bfloat16)

    def forward(block):
        ratios(block, rounded, rows_done, ratio)
        for at, (low, high, offset) in enumerate(blocks):
            turned = dot(ratio[:, low:high], x_back[offset : offset + high - low, :])
            back[rows_of(block, RADIUS), pl.ds(at * PART, PART)] = turned.astype(jnp.bfloat16)

    def update(block):
        for unit in range(UNIT):
            rows = pl.ds(pl.multiple_of(block * TALL + unit * BRICK, BRICK), BRICK)
            fresh = observed[rows, :] * dot(y_back[...], back[window(block, unit), :])
            estimate[rows, :] = fresh[:, HALO : HALO + PART]
            target = pl.ds(pl.multiple_of(block * TALL + unit * BRICK + RADIUS, RADIUS), BRICK)
            rounded_2[target, :] = fresh.astype(jnp.bfloat16)

    def again(block):
        ratios(block, rounded_2, rows_done_2, ratio_2)
        back_2[rows_of(block, RADIUS), :] = dot(ratio_2[...], x_back[...]).astype(jnp.bfloat16)

    def finish(block):
        for unit in range(UNIT):
            rows = pl.ds(pl.multiple_of(block * TALL + unit * BRICK, BRICK), BRICK)
            correction = dot(y_back[...], back_2[window(block, unit), :])
            final = estimate[rows, :] * correction
            coded[block * UNIT + unit] = (final * final).astype(jnp.bfloat16)

    def target(place, part):
        return whole.at[place, :, pl.ds(pl.multiple_of(part * PART, PART), PART)]

    keep = pltpu.make_async_copy(coded.at[spot], target(plane % 4, part), own.at[1])

    def leave(brick):
        return pltpu.make_async_remote_copy(
            src_ref=coded.at[brick],
            dst_ref=target(plane % 4, part),
            send_sem=send.at[brick],
            recv_sem=recv.at[plane % 4, part],
            device_id={"scan": group, "ybrick": brick},
            device_id_type=MESH,
        )

    def ship(block):
        for unit in range(UNIT):
            brick = block * UNIT + (unit + start_of(scan, spot)) % UNIT
            away = (stays == 0) | (brick != spot)

            @pl.when(away)
            def _():
                leave(brick).start()

            @pl.when(jnp.logical_not(away))
            def _():
                keep.start()

    for turn in (-1, 0, 1):
        await_halo(block_at(turn))
        load(block_at(turn))

    stages = (
        (await_halo, -2, 0, BLOCKS - 4),
        (ship, 7, 10, BLOCKS + 9),
        (finish, 6, 9, BLOCKS + 8),
        (again, 4, 6, BLOCKS + 5),
        (update, 2, 3, BLOCKS + 2),
        (forward, 0, 0, BLOCKS - 1),
        (load, -2, 0, BLOCKS - 4),
    )
    cuts = sorted({begin for _, _, begin, _ in stages} | {end + 1 for _, _, _, end in stages})
    for low, high in zip(cuts, cuts[1:]):
        active = [(stage, lag) for stage, lag, begin, end in stages if begin <= low and low <= end]

        def step(turn, carry):
            for stage, lag in active:
                stage(block_at(turn - lag))
            return carry

        lax.fori_loop(low, high, step, 0)

    def sent_raw(step, carry):
        fetch(step).wait_send()
        return carry

    def sent_halo(block, carry):
        both_halos(lambda one: one.wait_send(), block)
        return carry

    def sent(brick, carry):
        @pl.when((stays == 0) | (brick != spot))
        def _():
            leave(brick).wait_send()

        return carry

    lax.fori_loop(1, BRICKS, sent_raw, 0)
    lax.fori_loop(0, BLOCKS, sent_halo, 0)

    @pl.when(stays == 1)
    def _():
        keep.wait()

    lax.fori_loop(0, BRICKS, sent, 0)
    for place in range(4):
        for column in range(8):

            @pl.when((stays == 0) | (place != plane % 4) | (column != part))
            def _():
                ref = target(place, column)
                pltpu.make_async_copy(ref, ref, recv.at[place, column]).wait()


def deconvolve(raw, row_shift, frac_index, psf_y, psf_x):
    scratch = (
        ((1, WIDE), jnp.float32),
        ((BRICK, SPAN), jnp.bfloat16),
        ((BRICK, SPAN), jnp.bfloat16),
        ((WIDE, PART), jnp.bfloat16),
        ((WIDE, PART), jnp.bfloat16),
        ((REACH + ROWS, PART), jnp.bfloat16),
        ((BRICK, REACH + BRICK), jnp.bfloat16),
        ((ROWS, PART), jnp.bfloat16),
        ((ROWS, WIDE), jnp.float32),
        ((ROWS, PART), jnp.float32),
        ((ROWS + 2 * RADIUS, WIDE), jnp.bfloat16),
        ((ROWS + 2 * RADIUS, WIDE), jnp.bfloat16),
        ((ROWS + 2 * RADIUS, WIDE), jnp.bfloat16),
        ((ROWS + 2 * RADIUS, PART), jnp.bfloat16),
        ((TALL, WIDE), jnp.bfloat16),
        ((TALL, WIDE), jnp.bfloat16),
        ((TALL, WIDE), jnp.bfloat16),
        ((TALL, WIDE), jnp.bfloat16),
        ((BRICKS, BRICK, PART), jnp.bfloat16),
        ((ROWS, HALO), jnp.bfloat16),
        ((ROWS, HALO), jnp.bfloat16),
    )
    semaphores = ((BRICKS,), (BRICKS,), (2, BLOCKS), (2, BLOCKS), (BRICKS,), (4, 8), (2,))
    return pl.pallas_call(
        filter_kernel,
        out_shape=jax.ShapeDtypeStruct((4, BRICK, 8 * PART), jnp.bfloat16),
        in_specs=[REFS, SMEM, SMEM, VMEM, VMEM],
        out_specs=REFS,
        scratch_shapes=[pltpu.VMEM(*one) for one in scratch] + [pltpu.SemaphoreType.DMA(one) for one in semaphores],
        compiler_params=pltpu.CompilerParams(
            collective_id=0, has_side_effects=True, vmem_limit_bytes=60 * 2**20
        ),
    )(raw, row_shift, frac_index, psf_y.reshape(1, TAPS), psf_x.reshape(1, TAPS))


PIECES = 8


def decode_kernel(coded, out, before, after, arrive, leave):
    tall = 4 * BRICK // PIECES

    def piece(ref, k):
        return ref.at[k * tall // BRICK, pl.ds(k * tall % BRICK, tall), :]

    reads = [pltpu.make_async_copy(piece(coded, k), before.at[k], arrive.at[k]) for k in range(PIECES)]
    writes = [pltpu.make_async_copy(after.at[k], piece(out, k), leave.at[k]) for k in range(PIECES)]
    for read in reads:
        read.start()
    for k in range(PIECES):
        reads[k].wait()
        values = before[k].astype(jnp.float32)
        after[k] = values * lax.rsqrt(values)
        writes[k].start()
    for write in writes:
        write.wait()


def decode(coded):
    shape = (PIECES, 4 * BRICK // PIECES, 8 * PART)
    return pl.pallas_call(
        decode_kernel,
        out_shape=jax.ShapeDtypeStruct(coded.shape, jnp.float32),
        in_specs=[REFS],
        out_specs=REFS,
        scratch_shapes=[
            pltpu.VMEM(shape, jnp.bfloat16),
            pltpu.VMEM(shape, jnp.float32),
            pltpu.SemaphoreType.DMA((PIECES,)),
            pltpu.SemaphoreType.DMA((PIECES,)),
        ],
        compiler_params=pltpu.CompilerParams(vmem_limit_bytes=60 * 2**20),
    )(coded)


def local(raw, row_shift, frac_index, psf_y, psf_x):
    return decode(deconvolve(raw, row_shift, frac_index, psf_y, psf_x))


def solution(mesh):
    return jax.shard_map(
        local,
        mesh=mesh,
        in_specs=(P(None, "ybrick", "scan"), P(), P(), P(), P()),
        out_specs=P("scan", "ybrick", None),
        check_vma=False,
    )
```

```python
import functools

import jax
import jax.numpy as jnp
from jax import lax
from jax.experimental import pallas as pl
from jax.experimental.pallas import tpu as pltpu
from jax.sharding import PartitionSpec as P

RADIUS = 32
TAPS = 2 * RADIUS + 1
NFRAC = 16
BRICK = 128
BRICKS = 32
ROWS = BRICK * BRICKS
REACH = 1024
PART = 256
HALO = 128
WIDE = PART + 2 * HALO
SPAN = BRICK + 2 * RADIUS
UNIT = 2
TALL = UNIT * BRICK
BLOCKS = BRICKS // UNIT
STRIDE = 7
TINY = 1e-30
MESH = pl.DeviceIdType.MESH
SMEM = pl.BlockSpec(memory_space=pltpu.SMEM)
VMEM = pl.BlockSpec(memory_space=pltpu.VMEM)
REFS = pl.BlockSpec(memory_space=pl.ANY)

background = 0.5


def spot_of(plane, side, scan):
    deep, down, high = plane // 8, (plane // 2) % 4, plane % 2
    return high * 16 + down * 4 + (2 * deep + scan + side) % 4


def work_of(scan, ybrick):
    turn = (ybrick % 4 - scan + 4) % 4
    return 8 * (turn // 2) + 2 * ((ybrick % 16) // 4) + ybrick // 16, turn % 2


def start_of(scan, ybrick):
    plane, side = work_of(scan, ybrick)
    high, down = ybrick // 16, (ybrick // 4) % 2
    return (plane % 4) * 8 + 2 * scan + side


def spread(line, height, width, first):
    rows = jnp.broadcast_to(line[:, :width], (height, width))
    return pltpu.roll(rows, first % width, 1, stride=1, stride_axis=0)


def bands(psf_y, psf_x, line, y_forward, y_back, x_forward, x_back):
    line[...] = jnp.zeros_like(line)
    line[:, :TAPS] = psf_y[...] / jnp.sum(psf_y[...], axis=1, keepdims=True)
    y_forward[...] = spread(line, BRICK, 2 * BRICK, 0)[:, :SPAN].astype(jnp.bfloat16)
    turned = spread(line, 2 * BRICK, 2 * BRICK, -2 * RADIUS)[:, :BRICK].T
    y_back[...] = turned[:, :SPAN].astype(jnp.bfloat16)
    line[:, :TAPS] = psf_x[...] / jnp.sum(psf_x[...], axis=1, keepdims=True)
    x_forward[...] = spread(line, PART, WIDE, HALO - RADIUS).T.astype(jnp.bfloat16)
    x_back[...] = spread(line, WIDE, WIDE, -(HALO + RADIUS))[:, :PART].astype(jnp.bfloat16)


def filter_kernel(
    raw, row_shift, frac_index, psf_y, psf_x, whole,
    line, y_forward, y_back, x_forward, x_back, slots, moves, middle,
    observed, estimate, rounded, back, rounded_2, back_2, rows_done, ratio, rows_done_2, ratio_2,
    coded, left, right, raw_send, raw_recv, halo_send, halo_recv, send, recv, own,
):
    scan, spot = lax.axis_index("scan"), lax.axis_index("ybrick")
    plane, side = work_of(scan, spot)
    group, part = plane // 4, 2 * scan + side
    stays = (group == scan).astype(jnp.int32)
    first = start_of(scan, spot) // UNIT
    has_left, has_right = part > 0, part < 7

    def owner(plane, part):
        return {"scan": part // 2, "ybrick": spot_of(plane, part % 2, part // 2)}

    barrier = pltpu.get_barrier_semaphore()

    for there, step in ((has_left, -1), (has_right, 1)):

        @pl.when(there)
        def _():
            pl.semaphore_signal(barrier, inc=1, device_id=owner(plane, part + step), device_id_type=MESH)

    def greet_scan(step, carry):
        other = (spot + step) % BRICKS
        pl.semaphore_signal(barrier, inc=1, device_id={"ybrick": other}, device_id_type=MESH)
        return carry

    lax.fori_loop(1, BRICKS, greet_scan, 0)
    for from_scan in range(4):
        for turned in range(2):
            column = 2 * from_scan + turned
            deep = (2 * (scan // 2) + from_scan + turned) % 4
            for place in range(4):
                there = (place % 2) * 16 + (2 * (scan % 2) + place // 2) * 4 + deep

                @pl.when((from_scan != scan) | (there != spot))
                def _():
                    device = {"scan": from_scan, "ybrick": there}
                    pl.semaphore_signal(barrier, inc=1, device_id=device, device_id_type=MESH)

    pl.semaphore_wait(barrier, 2 * BRICKS - 1 - stays + has_left.astype(jnp.int32) + has_right.astype(jnp.int32))

    def source(there):
        its_plane, its_side = work_of(scan, there)
        return raw.at[its_plane, :, pl.ds(pl.multiple_of(its_side * PART, PART), PART)]

    def tile_of(brick):
        return slots.at[pl.ds(pl.multiple_of(REACH + brick * BRICK, BRICK), BRICK), :]

    keep_raw = pltpu.make_async_copy(source(spot), tile_of(spot), own.at[0])
    keep_raw.start()

    def fetch(step):
        there = (spot + STRIDE * step) % BRICKS
        return pltpu.make_async_remote_copy(
            src_ref=source(there),
            dst_ref=tile_of(spot),
            send_sem=raw_send.at[there],
            recv_sem=raw_recv.at[spot],
            device_id={"ybrick": there},
            device_id_type=MESH,
        )

    def start_fetch(step, carry):
        fetch(step).start()
        return carry

    lax.fori_loop(1, BRICKS, start_fetch, 0)
    bands(psf_y, psf_x, line, y_forward, y_back, x_forward, x_back)

    def block_at(turn):
        return (first + turn + BLOCKS) % BLOCKS

    def rows_of(block, offset=0):
        return pl.ds(pl.multiple_of(block * TALL + offset, RADIUS), TALL)

    def halo(block, to_right):
        edge = middle.at[rows_of(block), pl.ds(HALO if to_right else 0, HALO)]
        return pltpu.make_async_remote_copy(
            src_ref=edge,
            dst_ref=(left if to_right else right).at[rows_of(block), :],
            send_sem=halo_send.at[int(to_right), block],
            recv_sem=halo_recv.at[int(to_right), block],
            device_id=owner(plane, part + (1 if to_right else -1)),
            device_id_type=MESH,
        )

    def both_halos(act, block):
        for there, to_right in ((has_left, False), (has_right, True)):

            @pl.when(there)
            def _():
                act(halo(block, to_right))

    for ref in (rounded, back, rounded_2, back_2):
        for edge in (pl.ds(0, RADIUS), pl.ds(RADIUS + ROWS, RADIUS)):
            ref[edge, :] = jnp.zeros((RADIUS, ref.shape[1]), jnp.bfloat16)

    slots[pl.ds(0, REACH), :] = jnp.zeros((REACH, PART), jnp.bfloat16)
    weight = frac_index[plane].astype(jnp.float32) / NFRAC
    ahead = lax.broadcasted_iota(jnp.int32, moves.shape, 1) - lax.broadcasted_iota(jnp.int32, moves.shape, 0)
    upper = jnp.where(ahead == REACH - row_shift[plane], 1.0 - weight, 0.0)
    lower = jnp.where(ahead == REACH - 1 - row_shift[plane], weight, 0.0)
    moves[...] = (upper + lower).astype(jnp.bfloat16)
    keep_raw.wait()

    def arrive_raw(step, carry):
        brick = (spot - STRIDE * step + STRIDE * BRICKS) % BRICKS
        pltpu.make_async_copy(tile_of(brick), tile_of(brick), raw_recv.at[brick]).wait()
        return carry

    lax.fori_loop(1, BRICKS, arrive_raw, 0)

    def deskew(block):
        for unit in range(UNIT):
            begin = pl.multiple_of((block * UNIT + unit) * BRICK, BRICK)
            mixed = jnp.dot(moves[...], slots[pl.ds(begin, REACH + BRICK), :], preferred_element_type=jnp.float32)
            middle[pl.ds(begin, BRICK), :] = mixed.astype(jnp.bfloat16)

    def deskew_four(turn, carry):
        for at in range(4):
            both_halos(lambda one: one.start(), block_at(4 * turn + at + BLOCKS - 6))
        for at in range(4):
            deskew(block_at(4 * turn + at + BLOCKS - 2))
        return carry

    for at in range(4):
        deskew(block_at(at + BLOCKS - 2))
    lax.fori_loop(1, BLOCKS // 4, deskew_four, 0)
    for at in range(4):
        both_halos(lambda one: one.start(), block_at(at + 2 * BLOCKS - 6))

    def await_halo(block):
        rows = rows_of(block)
        for ref, arrived, inside in ((left, 1, has_left), (right, 0, has_right)):

            @pl.when(inside)
            def _():
                pltpu.make_async_copy(ref.at[rows, :], ref.at[rows, :], halo_recv.at[arrived, block]).wait()

    def load(block):
        rows = rows_of(block)
        for ref, at, width, inside in (
            (middle, HALO, PART, None),
            (left, 0, HALO, has_left),
            (right, HALO + PART, HALO, has_right),
        ):
            values = ref[rows, :].astype(jnp.float32) + background
            if inside is not None:
                values = jnp.where(inside, values, 0.0)
            observed[rows, pl.ds(at, width)] = values
            rounded[rows_of(block, RADIUS), pl.ds(at, width)] = values.astype(jnp.bfloat16)

    def dot(one, two):
        return jnp.dot(one, two, preferred_element_type=jnp.float32)

    def window(block, unit):
        return pl.ds(pl.multiple_of(block * TALL + unit * BRICK, BRICK), SPAN)

    blocks = ((0, 384, 128), (128, 512, 0))

    def ratios(block, source, rows_done, ratio):
        for unit in range(UNIT):
            rows_done[pl.ds(unit * BRICK, BRICK), :] = dot(
                y_forward[...], source[window(block, unit), :]
            ).astype(jnp.bfloat16)
        for at, (low, high, offset) in enumerate(blocks):
            blurred = dot(rows_done[:, low:high], x_forward[offset : offset + high - low, :])
            cut = pl.ds(at * PART, PART)
            ratio[:, cut] = (observed[rows_of(block), cut] / jnp.maximum(blurred, TINY)).astype(jnp.bfloat16)

    def forward(block):
        ratios(block, rounded, rows_done, ratio)
        for at, (low, high, offset) in enumerate(blocks):
            turned = dot(ratio[:, low:high], x_back[offset : offset + high - low, :])
            back[rows_of(block, RADIUS), pl.ds(at * PART, PART)] = turned.astype(jnp.bfloat16)

    def update(block):
        for unit in range(UNIT):
            rows = pl.ds(pl.multiple_of(block * TALL + unit * BRICK, BRICK), BRICK)
            fresh = observed[rows, :] * dot(y_back[...], back[window(block, unit), :])
            estimate[rows, :] = fresh[:, HALO : HALO + PART]
            target = pl.ds(pl.multiple_of(block * TALL + unit * BRICK + RADIUS, RADIUS), BRICK)
            rounded_2[target, :] = fresh.astype(jnp.bfloat16)

    def again(block):
        ratios(block, rounded_2, rows_done_2, ratio_2)
        back_2[rows_of(block, RADIUS), :] = dot(ratio_2[...], x_back[...]).astype(jnp.bfloat16)

    def finish(block):
        for unit in range(UNIT):
            rows = pl.ds(pl.multiple_of(block * TALL + unit * BRICK, BRICK), BRICK)
            correction = dot(y_back[...], back_2[window(block, unit), :])
            final = estimate[rows, :] * correction
            coded[block * UNIT + unit] = (final * final).astype(jnp.bfloat16)

    def target(place, part):
        return whole.at[place, :, pl.ds(pl.multiple_of(part * PART, PART), PART)]

    keep = pltpu.make_async_copy(coded.at[spot], target(plane % 4, part), own.at[1])

    def leave(brick):
        return pltpu.make_async_remote_copy(
            src_ref=coded.at[brick],
            dst_ref=target(plane % 4, part),
            send_sem=send.at[brick],
            recv_sem=recv.at[plane % 4, part],
            device_id={"scan": group, "ybrick": brick},
            device_id_type=MESH,
        )

    def ship(block):
        for unit in range(UNIT):
            brick = block * UNIT + (unit + start_of(scan, spot)) % UNIT
            away = (stays == 0) | (brick != spot)

            @pl.when(away)
            def _():
                leave(brick).start()

            @pl.when(jnp.logical_not(away))
            def _():
                keep.start()

    for turn in (-1, 0, 1):
        await_halo(block_at(turn))
        load(block_at(turn))

    stages = (
        (await_halo, -2, 0, BLOCKS - 4),
        (ship, 7, 10, BLOCKS + 9),
        (finish, 6, 9, BLOCKS + 8),
        (again, 4, 6, BLOCKS + 5),
        (update, 2, 3, BLOCKS + 2),
        (forward, 0, 0, BLOCKS - 1),
        (load, -2, 0, BLOCKS - 4),
    )
    cuts = sorted({begin for _, _, begin, _ in stages} | {end + 1 for _, _, _, end in stages})
    for low, high in zip(cuts, cuts[1:]):
        active = [(stage, lag) for stage, lag, begin, end in stages if begin <= low and low <= end]

        def step(turn, carry):
            for stage, lag in active:
                stage(block_at(turn - lag))
            return carry

        lax.fori_loop(low, high, step, 0)

    def sent_raw(step, carry):
        fetch(step).wait_send()
        return carry

    def sent_halo(block, carry):
        both_halos(lambda one: one.wait_send(), block)
        return carry

    def sent(brick, carry):
        @pl.when((stays == 0) | (brick != spot))
        def _():
            leave(brick).wait_send()

        return carry

    lax.fori_loop(1, BRICKS, sent_raw, 0)
    lax.fori_loop(0, BLOCKS, sent_halo, 0)

    @pl.when(stays == 1)
    def _():
        keep.wait()

    lax.fori_loop(0, BRICKS, sent, 0)
    for place in range(4):
        for column in range(8):

            @pl.when((stays == 0) | (place != plane % 4) | (column != part))
            def _():
                ref = target(place, column)
                pltpu.make_async_copy(ref, ref, recv.at[place, column]).wait()


def deconvolve(raw, row_shift, frac_index, psf_y, psf_x):
    scratch = (
        ((1, WIDE), jnp.float32),
        ((BRICK, SPAN), jnp.bfloat16),
        ((BRICK, SPAN), jnp.bfloat16),
        ((WIDE, PART), jnp.bfloat16),
        ((WIDE, PART), jnp.bfloat16),
        ((REACH + ROWS, PART), jnp.bfloat16),
        ((BRICK, REACH + BRICK), jnp.bfloat16),
        ((ROWS, PART), jnp.bfloat16),
        ((ROWS, WIDE), jnp.float32),
        ((ROWS, PART), jnp.float32),
        ((ROWS + 2 * RADIUS, WIDE), jnp.bfloat16),
        ((ROWS + 2 * RADIUS, WIDE), jnp.bfloat16),
        ((ROWS + 2 * RADIUS, WIDE), jnp.bfloat16),
        ((ROWS + 2 * RADIUS, PART), jnp.bfloat16),
        ((TALL, WIDE), jnp.bfloat16),
        ((TALL, WIDE), jnp.bfloat16),
        ((TALL, WIDE), jnp.bfloat16),
        ((TALL, WIDE), jnp.bfloat16),
        ((BRICKS, BRICK, PART), jnp.bfloat16),
        ((ROWS, HALO), jnp.bfloat16),
        ((ROWS, HALO), jnp.bfloat16),
    )
    semaphores = ((BRICKS,), (BRICKS,), (2, BLOCKS), (2, BLOCKS), (BRICKS,), (4, 8), (2,))
    return pl.pallas_call(
        filter_kernel,
        out_shape=jax.ShapeDtypeStruct((4, BRICK, 8 * PART), jnp.bfloat16),
        in_specs=[REFS, SMEM, SMEM, VMEM, VMEM],
        out_specs=REFS,
        scratch_shapes=[pltpu.VMEM(*one) for one in scratch] + [pltpu.SemaphoreType.DMA(one) for one in semaphores],
        compiler_params=pltpu.CompilerParams(
            collective_id=0, has_side_effects=True, vmem_limit_bytes=60 * 2**20
        ),
    )(raw, row_shift, frac_index, psf_y.reshape(1, TAPS), psf_x.reshape(1, TAPS))


PIECES = 8


def decode_kernel(coded, out, before, after, arrive, leave):
    tall = 4 * BRICK // PIECES

    def piece(ref, k):
        return ref.at[k * tall // BRICK, pl.ds(k * tall % BRICK, tall), :]

    reads = [pltpu.make_async_copy(piece(coded, k), before.at[k], arrive.at[k]) for k in range(PIECES)]
    writes = [pltpu.make_async_copy(after.at[k], piece(out, k), leave.at[k]) for k in range(PIECES)]
    for read in reads:
        read.start()
    for k in range(PIECES):
        reads[k].wait()
        values = before[k].astype(jnp.float32)
        after[k] = values * lax.rsqrt(values)
        writes[k].start()
    for write in writes:
        write.wait()


def decode(coded):
    shape = (PIECES, 4 * BRICK // PIECES, 8 * PART)
    return pl.pallas_call(
        decode_kernel,
        out_shape=jax.ShapeDtypeStruct(coded.shape, jnp.float32),
        in_specs=[REFS],
        out_specs=REFS,
        scratch_shapes=[
            pltpu.VMEM(shape, jnp.bfloat16),
            pltpu.VMEM(shape, jnp.float32),
            pltpu.SemaphoreType.DMA((PIECES,)),
            pltpu.SemaphoreType.DMA((PIECES,)),
        ],
        compiler_params=pltpu.CompilerParams(vmem_limit_bytes=60 * 2**20),
    )(coded)


def local(raw, row_shift, frac_index, psf_y, psf_x):
    return decode(deconvolve(raw, row_shift, frac_index, psf_y, psf_x))


def solution(mesh):
    return jax.shard_map(
        local,
        mesh=mesh,
        in_specs=(P(None, "ybrick", "scan"), P(), P(), P(), P()),
        out_specs=P("scan", "ybrick", None),
        check_vma=False,
    )
```
